256 devices in a mesh: gx: 4 (over y_lo, core), gy: 8 (over x, y_hi), gz: 8 (over z).
Axes of the slice: x: 4, y: 4 (y_hi: 2, y_lo: 2; y = y_hi * 2 + y_lo), z: 8, core: 2. Of those that a mesh axis runs over, the one named last changes fastest.
Arguments:
- tokens: bfloat16 [32, 64, 64, 256], P('gx', 'gy', 'gz'), may hold values from -6 to 6
- norm_gain: float32 [256], replicated, may hold values from 0.5 to 1.5
- query_weight: bfloat16 [256, 256], replicated, may hold values from -2 to 2
- key_weight: bfloat16 [256, 256], replicated, may hold values from -2 to 2
- value_weight: bfloat16 [256, 256], replicated, may hold values from -0.375 to 0.375
- head_scale: float32 [8], replicated, may hold values from 1 to 6
- out_weight: bfloat16 [256, 256], replicated, may hold values from -0.375 to 0.375
- mlp_gain: float32 [256], replicated, may hold values from 0.5 to 1.5
- up_weight: bfloat16 [256, 512], replicated, may hold values from -0.375 to 0.375
- down_weight: bfloat16 [512, 256], replicated, may hold values from -0.25 to 0.25
Outputs:
- layer_out: bfloat16 [32, 64, 64, 256], P('gx', 'gy', 'gz')
The draws below stay inside these ranges and needn't reach their ends.
All inputs are finite; a program needn't handle non-finite values.
Results may differ from the reference program's by a relative error of at most 0.0095.
Values may be sent and summed in bfloat16 or wider, within the bound.
A program may use at most 128 MiB of HBM per device.

```python
import math
import jax
import jax.numpy as jnp
from jax import lax

C = 256
HEADS = 8
HID = 512
TOK_DEV = 512
NX = 32
NY = 64
NZ = 64


def draw_key_weight(key, part):
    values = jax.random.normal(jax.random.fold_in(key, 21), (C, C), jnp.float32) / math.sqrt(C)
    return jnp.clip(values, -2.0, 2.0).astype(jnp.bfloat16)


def draw_query_weight(key, part):
    noise = jax.random.normal(jax.random.fold_in(key, 31), (C, C), jnp.float32) / math.sqrt(C)
    values = noise
    return jnp.clip(values, -2.0, 2.0).astype(jnp.bfloat16)


def draw_tokens(key, part):
    rough = jax.random.normal(jax.random.fold_in(key, 41), (NX, NY, NZ, C), jnp.float32)
    smooth = jax.random.normal(jax.random.fold_in(key, 43), (NX // 4, NY // 4, NZ // 4, C), jnp.float32)
    smooth = jnp.repeat(jnp.repeat(jnp.repeat(smooth, 4, axis=0), 4, axis=1), 4, axis=2)
    values = smooth + rough
    return jnp.clip(values, -6.0, 6.0).astype(jnp.bfloat16)


def normal_values(stream_key, dims, scale, most, held_as=jnp.bfloat16):
    entries = jax.random.normal(stream_key, dims, jnp.float32) * scale
    return jnp.minimum(jnp.maximum(entries, -most), most).astype(held_as)


def setup_inputs(seed: int = 0) -> dict:
    arg_keys = jax.random.split(jax.random.key(seed), 11)
    return {
        "tokens": draw_tokens(jax.random.fold_in(arg_keys[10], 71), 0),
        "norm_gain": jnp.clip(1.0 + 0.1 * jax.random.normal(arg_keys[1], (C,), jnp.float32), 0.5, 1.5),
        "query_weight": draw_query_weight(jax.random.fold_in(arg_keys[10], 71), 0),
        "key_weight": draw_key_weight(jax.random.fold_in(arg_keys[10], 71), 0),
        "value_weight": normal_values(arg_keys[4], (C, C), C ** -0.5, 0.375),
        "head_scale": jnp.clip(jnp.exp(jax.random.uniform(arg_keys[5], (HEADS,), jnp.float32, math.log(1.0), math.log(6.0))), 1.0, 6.0),
        "out_weight": normal_values(arg_keys[6], (C, C), C ** -0.5, 0.375),
        "mlp_gain": jnp.clip(1.0 + 0.1 * jax.random.normal(arg_keys[7], (C,), jnp.float32), 0.5, 1.5),
        "up_weight": normal_values(arg_keys[8], (C, HID), C ** -0.5, 0.375),
        "down_weight": normal_values(arg_keys[9], (HID, C), HID ** -0.5, 0.25),
    }


EPSILON = 1e-05

def layer_norm(values, gain):
    widened = values.astype(jnp.float32)
    average = lax.optimization_barrier(jnp.mean(widened, axis=-1, keepdims=True))
    centered = widened - average
    variance = lax.optimization_barrier(jnp.mean(centered * centered, axis=-1, keepdims=True))
    return (centered * lax.rsqrt(variance + EPSILON) * gain).astype(jnp.bfloat16)

def project(values, weight):
    flat = values.reshape(-1, values.shape[-1])
    result = jnp.dot(flat, weight, preferred_element_type=jnp.float32)
    return result.astype(jnp.bfloat16).reshape(values.shape[:-1] + (weight.shape[1],))

def pooled_mean(values, factor):
    extent = values.shape
    grouped = values.reshape(extent[0] // factor, factor, extent[1] // factor, factor, extent[2] // factor, factor, extent[3])
    return lax.optimization_barrier(jnp.mean(grouped, axis=(1, 3, 5), dtype=jnp.float32)).astype(jnp.bfloat16)

def wrap_pad(values):
    return jnp.pad(values, ((1, 1), (1, 1), (1, 1), (0, 0)), mode='wrap')

def unfold_axis(padded, dimension):
    windows = padded.shape[dimension] // 2 - 1
    paired = padded.reshape(padded.shape[:dimension] + (windows + 1, 2) + padded.shape[dimension + 1:])
    lower = lax.slice_in_dim(paired, 0, windows, axis=dimension)
    upper = lax.slice_in_dim(paired, 1, windows + 1, axis=dimension)
    return jnp.concatenate([lower, upper], axis=dimension + 1)

def unfold(padded):
    for dimension in (0, 2, 4):
        padded = unfold_axis(padded, dimension)
    return padded.transpose(0, 2, 4, 1, 3, 5, 6).reshape(padded.shape[0], padded.shape[2], padded.shape[4], 64, padded.shape[6])

def window_attend(key_pad, value_pad, queries, scaling):
    key_cells = unfold(key_pad)
    value_cells = unfold(value_pad)
    along_x, along_y, along_z, window_size, channels = key_cells.shape
    head_width = channels // HEADS
    query_side = queries.shape[0] // along_x
    windows = along_x * along_y * along_z
    grouped = queries.reshape(along_x, query_side, along_y, query_side, along_z, query_side, channels)
    grouped = grouped.transpose(0, 2, 4, 1, 3, 5, 6).reshape(windows, query_side ** 3, HEADS, head_width)
    key_cells = key_cells.reshape(windows, window_size, HEADS, head_width)
    value_cells = value_cells.reshape(windows, window_size, HEADS, head_width)
    scores = jnp.einsum('wqhd,wkhd->whqk', grouped.astype(jnp.float32), key_cells.astype(jnp.float32)) * scaling[None, :, None, None]
    highest = lax.optimization_barrier(jnp.max(scores, axis=-1, keepdims=True))
    weights = jnp.exp(scores - highest)
    summed = lax.optimization_barrier(jnp.sum(weights, axis=-1, keepdims=True))
    rounded = lax.optimization_barrier(weights.astype(jnp.bfloat16)).astype(jnp.float32)
    blended = jnp.einsum('whqk,wkhd->wqhd', rounded, value_cells.astype(jnp.float32))
    blended = blended / jnp.transpose(summed, (0, 2, 1, 3))
    blended = blended.reshape(along_x, along_y, along_z, query_side, query_side, query_side, channels)
    return blended.transpose(0, 3, 1, 4, 2, 5, 6).reshape(queries.shape)

def level_attend(key_pad, value_pad, queries, scaling):
    window_rows = (key_pad.shape[0] - 2) // 2
    query_side = queries.shape[0] // window_rows

    def one_row(row_index):
        key_slab = lax.dynamic_slice_in_dim(key_pad, (2 * row_index).astype(jnp.int32), 4, 0)
        value_slab = lax.dynamic_slice_in_dim(value_pad, (2 * row_index).astype(jnp.int32), 4, 0)
        query_slab = lax.dynamic_slice_in_dim(queries, (query_side * row_index).astype(jnp.int32), query_side, 0)
        return window_attend(key_slab, value_slab, query_slab, scaling)
    stacked = lax.map(one_row, jnp.arange(window_rows, dtype=jnp.int32))
    return stacked.reshape(queries.shape)

def coarse_attend(query_rows, coarse_keys, coarse_values, scaling):
    channels = query_rows.shape[-1]
    head_width = channels // HEADS
    key_heads = coarse_keys.reshape(-1, HEADS, head_width).astype(jnp.float32)
    value_heads = coarse_values.reshape(-1, HEADS, head_width).astype(jnp.float32)

    def one_block(block_rows):
        query_heads = block_rows.reshape(-1, HEADS, head_width).astype(jnp.float32)
        scores = jnp.einsum('qhd,khd->hqk', query_heads, key_heads) * scaling[:, None, None]
        highest = lax.optimization_barrier(jnp.max(scores, axis=-1, keepdims=True))
        weights = jnp.exp(scores - highest)
        summed = lax.optimization_barrier(jnp.sum(weights, axis=-1, keepdims=True))
        rounded = lax.optimization_barrier(weights.astype(jnp.bfloat16)).astype(jnp.float32)
        blended = jnp.einsum('hqk,khd->qhd', rounded, value_heads) / jnp.transpose(summed, (1, 0, 2))
        return blended.reshape(block_rows.shape)
    stacked = lax.map(one_block, query_rows.reshape(-1, TOK_DEV, channels))
    return stacked.reshape(query_rows.shape)

def reference(tokens, norm_gain, query_weight, key_weight, value_weight, head_scale, out_weight, mlp_gain, up_weight, down_weight):
    channels = tokens.shape[-1]
    scaling = head_scale / math.sqrt(channels // HEADS)
    normed = layer_norm(tokens, norm_gain)
    queries = project(normed, query_weight)
    fine_out = level_attend(wrap_pad(project(normed, key_weight)), wrap_pad(project(normed, value_weight)), queries, scaling)
    middle = pooled_mean(normed, 2)
    middle_out = level_attend(wrap_pad(project(middle, key_weight)), wrap_pad(project(middle, value_weight)), queries, scaling)
    coarse = pooled_mean(normed, 4).reshape(-1, channels)
    coarse_out = coarse_attend(queries.reshape(-1, channels), project(coarse, key_weight), project(coarse, value_weight), scaling)
    attended = (fine_out + middle_out + coarse_out.reshape(tokens.shape)).astype(jnp.bfloat16)
    flat_tokens = tokens.reshape(-1, channels)
    residual = (flat_tokens.astype(jnp.float32) + jnp.dot(attended.reshape(-1, channels), out_weight, preferred_element_type=jnp.float32)).astype(jnp.bfloat16)
    second = layer_norm(residual, mlp_gain)
    hidden = jax.nn.gelu(jnp.dot(second, up_weight, preferred_element_type=jnp.float32), approximate=True).astype(jnp.bfloat16)
    output = residual.astype(jnp.float32) + jnp.dot(hidden, down_weight, preferred_element_type=jnp.float32)
    return output.astype(jnp.bfloat16).reshape(tokens.shape)
```

```python
import functools
import math

import jax
import jax.numpy as jnp
import numpy as np
from jax import lax
from jax.experimental import pallas as pl
from jax.experimental.pallas import tpu as pltpu
from jax.sharding import PartitionSpec as P

MESH = pl.DeviceIdType.MESH
BF = jnp.bfloat16
F32 = jnp.float32
HEADS = 8
EPSILON = 1e-05
LOG2E = math.log2(math.e)
NEG = -1e30

FACES = [(1, 0, 0), (-1, 0, 0), (0, 1, 0), (0, -1, 0), (0, 0, 1), (0, 0, -1)]
OTHERS = [
    (i, j, k)
    for i in (1, 0, -1)
    for j in (1, 0, -1)
    for k in (1, 0, -1)
    if abs(i) + abs(j) + abs(k) > 1
]
DIRS = FACES + OTHERS
PACKED = 800
SRC = 1024
MID_AT = 896


def slot(d):
    if d in FACES:
        return 80 * FACES.index(d), 80
    return 512 + 16 * OTHERS.index(d), 16


def packed_slot(d):
    start, rows = slot(d)
    return (start if start < 512 else start - 32), rows


AT_Z, AT_M, AT_MZ, KEYS = 800, 1120, 1312, 1408


def halo_row(x, y, z, n, middle):
    d = tuple(1 if c == 0 else -1 if c == n + 1 else 0 for c in (x, y, z))
    free = [c - 1 for c, e in zip((x, y, z), d) if e == 0]
    if not any(d):
        return MID_AT + (free[0] * n + free[1]) * n + free[2]
    start, rows = slot(d)
    at = 0
    for c in free:
        at = at * n + c
    return start + at + ((64 if rows == 80 else 8) if middle else 0)


def selection():
    pick = np.zeros((KEYS - AT_Z, SRC), np.float32)
    for by in range(4):
        for x in range(10):
            for yy in range(4):
                for s in range(2):
                    row = by * 80 + x * 8 + yy * 2 + s
                    pick[row, halo_row(x, 2 * by + yy, 9 * s, 8, False)] = 1
    for my in range(2):
        for x in range(6):
            for yy in range(4):
                for z in range(4):
                    row = AT_M - AT_Z + my * 96 + x * 16 + yy * 4 + z
                    pick[row, halo_row(x, 2 * my + yy, z + 1, 4, True)] = 1
                for s in range(2):
                    row = AT_MZ - AT_Z + my * 48 + x * 8 + yy * 2 + s
                    pick[row, halo_row(x, 2 * my + yy, 5 * s, 4, True)] = 1
    return pick


def window_mask():
    mask = np.full((8, 256), NEG, np.float32)
    for q in range(8):
        for lane in range(256):
            if lane < 128:
                at, low = lane % 8 + 1, 2 * (q // 2)
            elif lane < 160:
                at, low = 9 * (lane % 2), 2 * (q // 2)
            elif lane < 224:
                at, low = lane % 4 + 1, 2 * (q // 4)
            else:
                at, low = 5 * (lane % 2), 2 * (q // 4)
            if low <= at <= low + 3:
                mask[q, lane] = 0
    return mask


def dot(a, b):
    return jnp.dot(a, b, preferred_element_type=F32)


def dot_t(a, b):
    return lax.dot_general(a, b, (((1,), (1,)), ((), ())), preferred_element_type=F32)


def normalized(values, gain):
    average = jnp.mean(values, axis=-1, keepdims=True)
    centered = values - average
    variance = jnp.mean(centered * centered, axis=-1, keepdims=True)
    return (centered * lax.rsqrt(variance + EPSILON) * gain).astype(BF)


def cf_rows(cf, k):
    return jnp.concatenate([cf[c, pl.ds(k, 8, stride=4), :] for c in range(2)], axis=1)


def layer_kernel(
    tok_ref, gain_ref, wq_ref, wk_ref, wv_ref, scale_ref, wo_hbm, gain2_ref, up_hbm, down_hbm, pick_hbm, mask_ref,
    out_ref,
    nf, mf, tf, cf, stage, packed, src, zbuf, cbuf, abuf, qn, qm, kbuf, vbuf, fm, kc, va, sa, sb, ms, acc,
    wo_ref, up_ref, down_ref, pick_ref, wvt,
    load_sem, halo_send, halo_recv, z_send, z_recv, a_send, a_recv, b_send, b_recv, c_send, c_recv,
):
    gx, gy, gz = lax.axis_index("gx"), lax.axis_index("gy"), lax.axis_index("gz")
    core, ylow = lax.rem(gx, 2), lax.div(gx, 2)
    xpos, yhigh = lax.div(gy, 2), lax.rem(gy, 2)
    ypos = yhigh * 2 + ylow

    def chip(x, y):
        return (lax.rem(y, 2) * 2 + core, x * 2 + lax.div(y, 2), gz)

    near = [
        (lax.rem(gx + d[0] + 4, 4), lax.rem(gy + d[1] + 8, 8), lax.rem(gz + d[2] + 8, 8))
        for d in DIRS
    ]
    along_z = [(gx, gy, lax.rem(gz + k, 8)) for k in range(1, 8)]
    first = [chip(lax.rem(xpos + k * (1 - core), 4), lax.rem(ypos + k * core, 4)) for k in range(1, 4)]
    then = [chip(lax.rem(xpos + k * core, 4), lax.rem(ypos + k * (1 - core), 4)) for k in range(1, 4)]
    partner = (gx + 1 - 2 * core, gy, gz)

    barrier = pltpu.get_barrier_semaphore()
    greeted = near + along_z + first + then
    for peer in greeted:
        pl.semaphore_signal(barrier, inc=1, device_id=peer, device_id_type=MESH)

    loads = [
        pltpu.make_async_copy(a, b, load_sem.at[i])
        for i, (a, b) in enumerate(
            ((pick_hbm, pick_ref), (wo_hbm, wo_ref), (up_hbm, up_ref), (down_hbm, down_ref))
        )
    ]
    for load in loads:
        load.start()

    normed = normalized(tok_ref[...].astype(F32), gain_ref[...])
    widened = normed.astype(F32)
    for c in range(2):
        half = widened[:, c * 128 : c * 128 + 128]
        nf[c] = half
        pairs = jnp.sum(half.reshape(4, 2, 4, 2, 8, 128), axis=(1, 3))
        tf[c] = pairs.reshape(128, 128)
        mf[c] = ((tf[c, pl.ds(0, 64, stride=2), :] + tf[c, pl.ds(1, 64, stride=2), :]) * 0.125).astype(BF).astype(F32)
        cf[c] = jnp.sum(pairs.reshape(2, 2, 2, 2, 8, 128), axis=(1, 3)).reshape(32, 128)
    coarse = cf_rows(cf, 0)
    for k in range(1, 4):
        coarse = coarse + cf_rows(cf, k)
    zbuf[0] = (coarse * (1.0 / 64)).astype(BF)

    for d in DIRS:
        start, rows = packed_slot(d)
        x, y, z = (7 if c > 0 else 0 for c in d)
        mx, my, mz = (3 if c > 0 else 0 for c in d)
        axes = tuple(c != 0 for c in d)
        at = start + (64 if rows == 80 else 8)
        for c in range(2):
            if rows == 16:
                stage[c, start : start + 16, :] = jnp.zeros((16, 128), F32)
            if axes == (True, False, False):
                stage[c, start : start + 64, :] = nf[c, x * 64 : x * 64 + 64, :]
                stage[c, at : at + 16, :] = mf[c, mx * 16 : mx * 16 + 16, :]
            elif axes == (False, True, False):
                for i in range(8):
                    stage[c, start + i * 8 : start + i * 8 + 8, :] = nf[c, i * 64 + y * 8 : i * 64 + y * 8 + 8, :]
                for i in range(4):
                    stage[c, at + i * 4 : at + i * 4 + 4, :] = mf[c, i * 16 + my * 4 : i * 16 + my * 4 + 4, :]
            elif axes == (False, False, True):
                stage[c, start : start + 64, :] = nf[c, pl.ds(z, 64, stride=8), :]
                stage[c, at : at + 16, :] = mf[c, pl.ds(mz, 16, stride=4), :]
            elif axes == (True, True, False):
                stage[c, start : start + 8, :] = nf[c, x * 64 + y * 8 : x * 64 + y * 8 + 8, :]
                stage[c, at : at + 4, :] = mf[c, mx * 16 + my * 4 : mx * 16 + my * 4 + 4, :]
            elif axes == (True, False, True):
                stage[c, start : start + 8, :] = nf[c, pl.ds(x * 64 + z, 8, stride=8), :]
                stage[c, at : at + 4, :] = mf[c, pl.ds(mx * 16 + mz, 4, stride=4), :]
            elif axes == (False, True, True):
                stage[c, start : start + 8, :] = nf[c, pl.ds(y * 8 + z, 8, stride=64), :]
                stage[c, at : at + 4, :] = mf[c, pl.ds(my * 4 + mz, 4, stride=16), :]
            else:
                row, mrow = x * 64 + y * 8 + z, mx * 16 + my * 4 + mz
                stage[c, start : start + 1, :] = nf[c, row : row + 1, :]
                stage[c, at : at + 1, :] = mf[c, mrow : mrow + 1, :]
    packed[...] = jnp.concatenate([stage[0], stage[1]], axis=1).astype(BF)

    src[480:512, :] = jnp.zeros((32, 256), BF)
    src[832:896, :] = jnp.zeros((64, 256), BF)
    src[960:1024, :] = jnp.zeros((64, 256), BF)
    src[MID_AT : MID_AT + 64, :] = jnp.concatenate([mf[0], mf[1]], axis=1).astype(BF)

    pl.semaphore_wait(barrier, len(greeted))

    z_copies = [
        pltpu.make_async_remote_copy(
            src_ref=zbuf.at[0], dst_ref=zbuf.at[k], send_sem=z_send.at[k], recv_sem=z_recv.at[k],
            device_id=along_z[k - 1], device_id_type=MESH,
        )
        for k in range(1, 8)
    ]
    for copy in z_copies:
        copy.start()
    halo = []
    for i, d in enumerate(DIRS):
        start, rows = packed_slot(d)
        land, _ = slot(d)
        halo.append(
            pltpu.make_async_remote_copy(
                src_ref=packed.at[pl.ds(start, rows)], dst_ref=src.at[pl.ds(land, rows)],
                send_sem=halo_send.at[i], recv_sem=halo_recv.at[i], device_id=near[i], device_id_type=MESH,
            )
        )
    for copy in halo:
        copy.start()

    factor = LOG2E / math.sqrt(32)
    lane_head = lax.broadcasted_iota(jnp.int32, (1, 256), 1) // 32
    spread = jnp.zeros((1, 256), F32)
    for h in range(HEADS):
        spread = jnp.where(lane_head == h, scale_ref[h] * factor, spread)
    qn[...] = (dot(normed, wq_ref[...]) * spread).astype(BF)
    turned = dot_t(wq_ref[...].T, normed)
    qm[...] = jnp.zeros_like(qm)
    for h in range(HEADS):
        at = (h % 4) * 32
        qm[h, at : at + 32, :] = (turned[h * 32 : h * 32 + 32, :] * (scale_ref[h] * factor)).astype(BF)
    wvt[...] = wv_ref[...].T
    va[:, 32:48, :] = jnp.ones((HEADS, 16, 256), BF)
    ms[...] = jnp.full_like(ms, NEG)
    acc[...] = jnp.zeros_like(acc)

    for copy in z_copies:
        copy.wait()
    cbuf[0:64, :] = zbuf[...].astype(F32).reshape(64, 256).astype(BF)
    a_copies = [
        pltpu.make_async_remote_copy(
            src_ref=cbuf.at[pl.ds(0, 64)], dst_ref=cbuf.at[pl.ds(64 * k, 64)],
            send_sem=a_send.at[k], recv_sem=a_recv.at[k], device_id=first[k - 1], device_id_type=MESH,
        )
        for k in range(1, 4)
    ]
    for copy in a_copies:
        copy.start()

    for copy in halo:
        copy.wait()

    def cells(d, row):
        start, _ = slot(d)
        at = start + row
        low = at - at % 16
        tile = src[low : low + 16, :].astype(F32)
        return tile[at - low : at - low + 8, :]

    for x in range(10):
        ex = 1 if x == 0 else -1 if x == 9 else 0
        if ex:
            begin, end = cells((ex, 1, 0), 0), cells((ex, -1, 0), 0)
            start, _ = slot((ex, 0, 0))
            inner = src[start : start + 64, :].astype(F32)
        else:
            begin, end = cells((0, 1, 0), (x - 1) * 8), cells((0, -1, 0), (x - 1) * 8)
            own = slice((x - 1) * 64, x * 64)
            inner = jnp.concatenate([nf[0, own, :], nf[1, own, :]], axis=1)
        abuf[x * 80 : x * 80 + 80, :] = jnp.concatenate([begin, inner, end], axis=0).astype(BF)
    loads[0].wait()
    abuf[AT_Z:KEYS, :] = dot(pick_ref[...], src[...]).astype(BF)

    def project(i, carry):
        rows = pl.ds(pl.multiple_of(i * 128, 128), 128)
        a = abuf[rows, :]
        kbuf[rows, :] = dot(a, wk_ref[...]).astype(BF)
        vbuf[rows, :] = dot(a, wv_ref[...]).astype(BF)
        return carry

    lax.fori_loop(0, KEYS // 128, project, 0)

    for copy in a_copies:
        copy.wait()
    b_copies = [
        pltpu.make_async_remote_copy(
            src_ref=cbuf.at[pl.ds(0, 256)], dst_ref=cbuf.at[pl.ds(256 * k, 256)],
            send_sem=b_send.at[k], recv_sem=b_recv.at[k], device_id=then[k - 1], device_id_type=MESH,
        )
        for k in range(1, 4)
    ]
    for copy in b_copies:
        copy.start()
    c_copies = [
        pltpu.make_async_remote_copy(
            src_ref=cbuf.at[pl.ds(256 * k, 256)], dst_ref=cbuf.at[pl.ds(1024 + 256 * k, 256)],
            send_sem=c_send.at[k], recv_sem=c_recv.at[k], device_id=partner, device_id_type=MESH,
        )
        for k in range(4)
    ]
    c_copies[0].start()

    lane = lax.broadcasted_iota(jnp.int32, (1, 128), 1)
    is_fine = lane < 32

    def windows(g, carry):
        bx, by = lax.div(g, 4), lax.rem(g, 4)
        mx, my = lax.div(bx, 2), lax.div(by, 2)

        def rows(start, count):
            return pl.ds(pl.multiple_of(start, 16), count)

        r0 = rows(bx * 128 + by * 16, 16)
        r1 = rows(bx * 128 + by * 16 + 64, 16)
        parts = [rows((2 * bx + i) * 80 + by * 16, 32) for i in range(4)] + [
            rows(AT_Z + by * 80 + bx * 16, 32),
            rows(AT_M + my * 96 + mx * 32, 64),
            rows(AT_MZ + my * 48 + mx * 16, 32),
        ]
        q = jnp.concatenate([qn[r0, :], qn[r1, :]], axis=0)
        spread_q = jnp.concatenate(
            [jnp.where(lane_head == h, q, jnp.zeros_like(q)) for h in range(HEADS)], axis=0
        )
        keys = jnp.concatenate([kbuf[p, :] for p in parts], axis=0)
        values = jnp.concatenate([vbuf[p, :] for p in parts], axis=0)
        scores = (dot_t(spread_q, keys).reshape(32, 8, 256) + mask_ref[...][None]).reshape(256, 256)
        s0, s1 = scores[:, :128], scores[:, 128:]
        top_f = jnp.max(jnp.maximum(s0, jnp.where(is_fine, s1, NEG)), axis=1, keepdims=True)
        top_m = jnp.max(jnp.where(is_fine, NEG, s1), axis=1, keepdims=True)
        e0 = jnp.exp2(s0 - top_f)
        e1 = jnp.exp2(s1 - jnp.where(is_fine, top_f, top_m))
        sum_f = jnp.sum(e0 + jnp.where(is_fine, e1, 0.0), axis=1, keepdims=True)
        sum_m = jnp.sum(jnp.where(is_fine, 0.0, e1), axis=1, keepdims=True)
        inv_f, inv_m = 1.0 / sum_f, 1.0 / sum_m
        weights = jnp.concatenate([e0 * inv_f, e1 * jnp.where(is_fine, inv_f, inv_m)], axis=1).astype(BF)
        mixed = dot(weights, values)
        total = jnp.zeros((32, 256), F32)
        for h in range(HEADS):
            total = jnp.where(lane_head == h, mixed[h * 32 : h * 32 + 32, :], total)
        fm[r0, :] = total[:16]
        fm[r1, :] = total[16:]
        return carry

    lax.fori_loop(0, 16, windows, 0)

    def scores_of(h, into):
        s = dot(kc[h // 4], qm[h])
        into[...] = s
        return jnp.max(s, axis=0, keepdims=True)

    def absorb(h, held, block_top):
        old = ms[h : h + 1, :]
        top = jnp.maximum(old, block_top)
        p = jnp.exp2(held[...] - top).astype(BF)
        acc[h] = acc[h] * jnp.exp2(old - top) + dot(va[h], p)
        ms[h : h + 1, :] = top

    def coarse_block(j, carry):
        s, other = lax.div(j, 2), lax.rem(j, 2)

        @pl.when(jnp.logical_and(other == 0, s > 0))
        def _():
            row = pl.multiple_of(256 * s, 256)
            pltpu.make_async_remote_copy(
                src_ref=cbuf.at[pl.ds(0, 256)], dst_ref=cbuf.at[pl.ds(row, 256)],
                send_sem=b_send.at[s], recv_sem=b_recv.at[s], device_id=then[0], device_id_type=MESH,
            ).wait_recv()
            pltpu.make_async_remote_copy(
                src_ref=cbuf.at[pl.ds(row, 256)], dst_ref=cbuf.at[pl.ds(1024 + row, 256)],
                send_sem=c_send.at[s], recv_sem=c_recv.at[s], device_id=partner, device_id_type=MESH,
            ).start()

        @pl.when(other == 1)
        def _():
            row = pl.multiple_of(256 * s, 256)
            pltpu.make_async_remote_copy(
                src_ref=cbuf.at[pl.ds(row, 256)], dst_ref=cbuf.at[pl.ds(1024 + row, 256)],
                send_sem=c_send.at[s], recv_sem=c_recv.at[s], device_id=partner, device_id_type=MESH,
            ).wait_recv()

        c = cbuf[pl.ds(pl.multiple_of(1024 * other + 256 * s, 256), 256), :]
        k = dot(c, wk_ref[...]).astype(BF)
        kc[0] = k[:, :128]
        kc[1] = k[:, 128:]
        v = dot_t(wvt[...], c).astype(BF)
        for h in range(HEADS):
            va[h, 0:32, :] = v[h * 32 : h * 32 + 32, :]
        held = (sa, sb)
        top = scores_of(0, sa)
        for h in range(HEADS):
            following = scores_of(h + 1, held[(h + 1) % 2]) if h + 1 < HEADS else None
            absorb(h, held[h % 2], top)
            top = following
        return carry

    lax.fori_loop(0, 8, coarse_block, 0)

    for load in loads[1:]:
        load.wait()
    turned_out = jnp.concatenate([acc[h, 0:32, :] / acc[h, 32:33, :] for h in range(HEADS)], axis=0)
    fm[...] = fm[...] + turned_out.T

    def finish(i, carry):
        rows = pl.ds(pl.multiple_of(i * 128, 128), 128)
        attended = fm[rows, :].astype(BF)
        residual = (tok_ref[rows, :].astype(F32) + dot(attended, wo_ref[...])).astype(BF)
        wide = residual.astype(F32)
        second = normalized(wide, gain2_ref[...])
        hidden = jax.nn.gelu(dot(second, up_ref[...]), approximate=True).astype(BF)
        out_ref[rows, :] = (wide + dot(hidden, down_ref[...])).astype(BF)
        return carry

    lax.fori_loop(0, 4, finish, 0)

    for copy in b_copies:
        copy.wait_send()
    for copy in c_copies:
        copy.wait_send()


def shards(
    tokens, norm_gain, query_weight, key_weight, value_weight, head_scale, out_weight, mlp_gain, up_weight, down_weight
):
    shape = tokens.shape
    vmem = pl.BlockSpec(memory_space=pltpu.VMEM)
    smem = pl.BlockSpec(memory_space=pltpu.SMEM)
    hbm = pl.BlockSpec(memory_space=pl.ANY)
    dma = pltpu.SemaphoreType.DMA
    V = pltpu.VMEM
    flat = pl.pallas_call(
        layer_kernel,
        out_shape=jax.ShapeDtypeStruct((512, 256), BF),
        in_specs=[vmem, vmem, vmem, vmem, vmem, smem, hbm, vmem, hbm, hbm, hbm, vmem],
        out_specs=vmem,
        scratch_shapes=[
            V((2, 512, 128), F32),
            V((2, 64, 128), F32),
            V((2, 128, 128), F32),
            V((2, 32, 128), F32),
            V((2, PACKED, 128), F32),
            V((PACKED, 256), BF),
            V((SRC, 256), BF),
            V((8, 8, 256), BF),
            V((2048, 256), BF),
            V((KEYS, 256), BF),
            V((512, 256), BF),
            V((8, 128, 512), BF),
            V((KEYS, 256), BF),
            V((KEYS, 256), BF),
            V((512, 256), F32),
            V((2, 256, 128), BF),
            V((8, 48, 256), BF),
            V((256, 512), F32),
            V((256, 512), F32),
            V((8, 512), F32),
            V((8, 48, 512), F32),
            V((256, 256), BF),
            V((256, 512), BF),
            V((512, 256), BF),
            V((KEYS - AT_Z, SRC), BF),
            V((256, 256), BF),
            dma((4,)),
            dma((26,)),
            dma((26,)),
            dma((8,)),
            dma((8,)),
            dma((4,)),
            dma((4,)),
            dma((4,)),
            dma((4,)),
            dma((4,)),
            dma((4,)),
        ],
        compiler_params=pltpu.CompilerParams(
            collective_id=0, has_side_effects=True, vmem_limit_bytes=60 << 20
        ),
        name="layer",
    )(
        tokens.reshape(512, 256),
        norm_gain.reshape(1, 256),
        query_weight,
        key_weight,
        value_weight,
        head_scale,
        out_weight,
        mlp_gain.reshape(1, 256),
        up_weight,
        down_weight,
        jnp.asarray(selection(), BF),
        jnp.asarray(window_mask()),
    )
    return flat.reshape(shape)


def solution(mesh):
    in_specs = (P("gx", "gy", "gz", None), P(), P(), P(), P(), P(), P(), P(), P(), P())
    step = jax.shard_map(shards, mesh=mesh, in_specs=in_specs, out_specs=P("gx", "gy", "gz", None), check_vma=False)

    def traced(*arguments):
        with jax.sharding.use_abstract_mesh(mesh.abstract_mesh):
            return step(*arguments)

    return traced
```

```python
import functools
import math

import jax
import jax.numpy as jnp
import numpy as np
from jax import lax
from jax.experimental import pallas as pl
from jax.experimental.pallas import tpu as pltpu
from jax.sharding import PartitionSpec as P

MESH = pl.DeviceIdType.MESH
BF = jnp.bfloat16
F32 = jnp.float32
HEADS = 8
EPSILON = 1e-05
LOG2E = math.log2(math.e)
NEG = -1e30
AHEAD = 3

FACES = [(1, 0, 0), (-1, 0, 0), (0, 1, 0), (0, -1, 0), (0, 0, 1), (0, 0, -1)]
OTHERS = [
    (i, j, k)
    for i in (1, 0, -1)
    for j in (1, 0, -1)
    for k in (1, 0, -1)
    if abs(i) + abs(j) + abs(k) > 1
]
DIRS = FACES + OTHERS
PACKED = 800
SRC = 1024
MID_AT = 896


def slot(d):
    if d in FACES:
        return 80 * FACES.index(d), 80
    return 512 + 16 * OTHERS.index(d), 16


def packed_slot(d):
    start, rows = slot(d)
    return (start if start < 512 else start - 32), rows


AT_Z, AT_M, AT_MZ, KEYS = 800, 1120, 1312, 1408


def halo_row(x, y, z, n, middle):
    d = tuple(1 if c == 0 else -1 if c == n + 1 else 0 for c in (x, y, z))
    free = [c - 1 for c, e in zip((x, y, z), d) if e == 0]
    if not any(d):
        return MID_AT + (free[0] * n + free[1]) * n + free[2]
    start, rows = slot(d)
    at = 0
    for c in free:
        at = at * n + c
    return start + at + ((64 if rows == 80 else 8) if middle else 0)


def selection():
    pick = np.zeros((KEYS - AT_Z, SRC), np.float32)
    for by in range(4):
        for x in range(10):
            for yy in range(4):
                for s in range(2):
                    row = by * 80 + x * 8 + yy * 2 + s
                    pick[row, halo_row(x, 2 * by + yy, 9 * s, 8, False)] = 1
    for my in range(2):
        for x in range(6):
            for yy in range(4):
                for z in range(4):
                    row = AT_M - AT_Z + my * 96 + x * 16 + yy * 4 + z
                    pick[row, halo_row(x, 2 * my + yy, z + 1, 4, True)] = 1
                for s in range(2):
                    row = AT_MZ - AT_Z + my * 48 + x * 8 + yy * 2 + s
                    pick[row, halo_row(x, 2 * my + yy, 5 * s, 4, True)] = 1
    return pick


def window_masks():
    mask = np.full((8, 384), NEG, np.float32)
    for q in range(8):
        for lane in range(256):
            if lane < 128:
                at, low, put = lane % 8 + 1, 2 * (q // 2), lane
            elif lane < 160:
                at, low, put = 9 * (lane % 2), 2 * (q // 2), lane
            elif lane < 224:
                at, low, put = lane % 4 + 1, 2 * (q // 4), lane + 128
            else:
                at, low, put = 5 * (lane % 2), 2 * (q // 4), lane + 128
            if low <= at <= low + 3:
                mask[q, put] = 0
    return mask


def dot(a, b):
    return jnp.dot(a, b, preferred_element_type=F32)


def dot_t(a, b):
    return lax.dot_general(a, b, (((1,), (1,)), ((), ())), preferred_element_type=F32)


def normalized(values, gain):
    average = jnp.mean(values, axis=-1, keepdims=True)
    centered = values - average
    variance = jnp.mean(centered * centered, axis=-1, keepdims=True)
    return (centered * lax.rsqrt(variance + EPSILON) * gain).astype(BF)


def cf_rows(cf, k):
    return jnp.concatenate([cf[c, pl.ds(k, 8, stride=4), :] for c in range(2)], axis=1)


def layer_kernel(
    tok_ref, gain_ref, wq_ref, wk_ref, wv_ref, scale_ref, wo_hbm, gain2_ref, up_hbm, down_hbm, pick_hbm, mask_ref,
    out_ref,
    nf, mf, tf, cf, stage, packed, src, zbuf, cbuf, abuf, qn, qm, kbuf, vbuf, wbuf, fm, kc, va, held, ms, acc,
    wo_ref, up_ref, down_ref, pick_ref, wvt,
    load_sem, halo_send, halo_recv, z_send, z_recv, a_send, a_recv, b_send, b_recv, c_send, c_recv,
):
    gx, gy, gz = lax.axis_index("gx"), lax.axis_index("gy"), lax.axis_index("gz")
    core, ylow = lax.rem(gx, 2), lax.div(gx, 2)
    xpos, yhigh = lax.div(gy, 2), lax.rem(gy, 2)
    ypos = yhigh * 2 + ylow

    def chip(x, y):
        return (lax.rem(y, 2) * 2 + core, x * 2 + lax.div(y, 2), gz)

    near = [
        (lax.rem(gx + d[0] + 4, 4), lax.rem(gy + d[1] + 8, 8), lax.rem(gz + d[2] + 8, 8))
        for d in DIRS
    ]
    along_z = [(gx, gy, lax.rem(gz + k, 8)) for k in range(1, 8)]
    first = [chip(lax.rem(xpos + k * (1 - core), 4), lax.rem(ypos + k * core, 4)) for k in range(1, 4)]
    then = [chip(lax.rem(xpos + k * core, 4), lax.rem(ypos + k * (1 - core), 4)) for k in (1, 3)]
    partner = (gx + 1 - 2 * core, gy, gz)

    barrier = pltpu.get_barrier_semaphore()
    greeted = near + along_z[1:6] + first + then
    for peer in greeted:
        pl.semaphore_signal(barrier, inc=1, device_id=peer, device_id_type=MESH)

    loads = [
        pltpu.make_async_copy(a, b, load_sem.at[i])
        for i, (a, b) in enumerate(
            ((pick_hbm, pick_ref), (wo_hbm, wo_ref), (up_hbm, up_ref), (down_hbm, down_ref))
        )
    ]
    for load in loads:
        load.start()

    normed = normalized(tok_ref[...].astype(F32), gain_ref[...])
    widened = normed.astype(F32)
    for c in range(2):
        half = widened[:, c * 128 : c * 128 + 128]
        nf[c] = half
        pairs = jnp.sum(half.reshape(4, 2, 4, 2, 8, 128), axis=(1, 3))
        tf[c] = pairs.reshape(128, 128)
        mf[c] = ((tf[c, pl.ds(0, 64, stride=2), :] + tf[c, pl.ds(1, 64, stride=2), :]) * 0.125).astype(BF).astype(F32)
        cf[c] = jnp.sum(pairs.reshape(2, 2, 2, 2, 8, 128), axis=(1, 3)).reshape(32, 128)
    coarse = cf_rows(cf, 0)
    for k in range(1, 4):
        coarse = coarse + cf_rows(cf, k)
    zbuf[0] = (coarse * (1.0 / 64)).astype(BF)

    for d in DIRS:
        start, rows = packed_slot(d)
        x, y, z = (7 if c > 0 else 0 for c in d)
        mx, my, mz = (3 if c > 0 else 0 for c in d)
        axes = tuple(c != 0 for c in d)
        at = start + (64 if rows == 80 else 8)
        for c in range(2):
            if rows == 16:
                stage[c, start : start + 16, :] = jnp.zeros((16, 128), F32)
            if axes == (True, False, False):
                stage[c, start : start + 64, :] = nf[c, x * 64 : x * 64 + 64, :]
                stage[c, at : at + 16, :] = mf[c, mx * 16 : mx * 16 + 16, :]
            elif axes == (False, True, False):
                for i in range(8):
                    stage[c, start + i * 8 : start + i * 8 + 8, :] = nf[c, i * 64 + y * 8 : i * 64 + y * 8 + 8, :]
                for i in range(4):
                    stage[c, at + i * 4 : at + i * 4 + 4, :] = mf[c, i * 16 + my * 4 : i * 16 + my * 4 + 4, :]
            elif axes == (False, False, True):
                stage[c, start : start + 64, :] = nf[c, pl.ds(z, 64, stride=8), :]
                stage[c, at : at + 16, :] = mf[c, pl.ds(mz, 16, stride=4), :]
            elif axes == (True, True, False):
                stage[c, start : start + 8, :] = nf[c, x * 64 + y * 8 : x * 64 + y * 8 + 8, :]
                stage[c, at : at + 4, :] = mf[c, mx * 16 + my * 4 : mx * 16 + my * 4 + 4, :]
            elif axes == (True, False, True):
                stage[c, start : start + 8, :] = nf[c, pl.ds(x * 64 + z, 8, stride=8), :]
                stage[c, at : at + 4, :] = mf[c, pl.ds(mx * 16 + mz, 4, stride=4), :]
            elif axes == (False, True, True):
                stage[c, start : start + 8, :] = nf[c, pl.ds(y * 8 + z, 8, stride=64), :]
                stage[c, at : at + 4, :] = mf[c, pl.ds(my * 4 + mz, 4, stride=16), :]
            else:
                row, mrow = x * 64 + y * 8 + z, mx * 16 + my * 4 + mz
                stage[c, start : start + 1, :] = nf[c, row : row + 1, :]
                stage[c, at : at + 1, :] = mf[c, mrow : mrow + 1, :]
    packed[...] = jnp.concatenate([stage[0], stage[1]], axis=1).astype(BF)

    src[480:512, :] = jnp.zeros((32, 256), BF)
    src[832:896, :] = jnp.zeros((64, 256), BF)
    src[960:1024, :] = jnp.zeros((64, 256), BF)
    src[MID_AT : MID_AT + 64, :] = jnp.concatenate([mf[0], mf[1]], axis=1).astype(BF)

    pl.semaphore_wait(barrier, len(greeted))

    z_copies = [
        pltpu.make_async_remote_copy(
            src_ref=zbuf.at[0], dst_ref=zbuf.at[k], send_sem=z_send, recv_sem=z_recv,
            device_id=along_z[k - 1], device_id_type=MESH,
        )
        for k in range(1, 8)
    ]
    for copy in z_copies:
        copy.start()
    halo = []
    for i, d in enumerate(DIRS):
        start, rows = packed_slot(d)
        land, _ = slot(d)
        halo.append(
            pltpu.make_async_remote_copy(
                src_ref=packed.at[pl.ds(start, rows)], dst_ref=src.at[pl.ds(land, rows)],
                send_sem=halo_send, recv_sem=halo_recv, device_id=near[i], device_id_type=MESH,
            )
        )
    for copy in halo:
        copy.start()

    factor = LOG2E / math.sqrt(32)
    lane_head = lax.broadcasted_iota(jnp.int32, (1, 256), 1) // 32
    spread = jnp.zeros((1, 256), F32)
    for h in range(HEADS):
        spread = jnp.where(lane_head == h, scale_ref[h] * factor, spread)
    qn[...] = (dot(normed, wq_ref[...]) * spread).astype(BF)
    turned = dot_t(wq_ref[...].T, normed)
    qm[...] = jnp.zeros_like(qm)
    for h in range(HEADS):
        at = (h % 4) * 32
        qm[h, at : at + 32, :] = (turned[h * 32 : h * 32 + 32, :] * (scale_ref[h] * factor)).astype(BF)
    wvt[...] = wv_ref[...].T
    va[:, 32:48, :] = jnp.ones((HEADS, 16, 256), BF)
    ms[...] = jnp.full_like(ms, NEG)
    acc[...] = jnp.zeros_like(acc)

    pltpu.make_async_remote_copy(
        src_ref=zbuf.at[pl.ds(1, 7)], dst_ref=zbuf.at[pl.ds(1, 7)], send_sem=z_send, recv_sem=z_recv,
        device_id=along_z[0], device_id_type=MESH,
    ).wait()
    cbuf[0:64, :] = zbuf[...].astype(F32).reshape(64, 256).astype(BF)
    a_copies = [
        pltpu.make_async_remote_copy(
            src_ref=cbuf.at[pl.ds(0, 64)], dst_ref=cbuf.at[pl.ds(64 * k, 64)],
            send_sem=a_send, recv_sem=a_recv, device_id=first[k - 1], device_id_type=MESH,
        )
        for k in range(1, 4)
    ]
    for copy in a_copies:
        copy.start()

    pltpu.make_async_remote_copy(
        src_ref=packed, dst_ref=packed, send_sem=halo_send, recv_sem=halo_recv,
        device_id=near[0], device_id_type=MESH,
    ).wait()

    def cells(d, row):
        start, _ = slot(d)
        at = start + row
        low = at - at % 16
        tile = src[low : low + 16, :].astype(F32)
        return tile[at - low : at - low + 8, :]

    for x in range(10):
        ex = 1 if x == 0 else -1 if x == 9 else 0
        if ex:
            begin, end = cells((ex, 1, 0), 0), cells((ex, -1, 0), 0)
            start, _ = slot((ex, 0, 0))
            inner = src[start : start + 64, :].astype(F32)
        else:
            begin, end = cells((0, 1, 0), (x - 1) * 8), cells((0, -1, 0), (x - 1) * 8)
            own = slice((x - 1) * 64, x * 64)
            inner = jnp.concatenate([nf[0, own, :], nf[1, own, :]], axis=1)
        abuf[x * 80 : x * 80 + 80, :] = jnp.concatenate([begin, inner, end], axis=0).astype(BF)
    loads[0].wait()
    abuf[AT_Z:KEYS, :] = dot(pick_ref[...], src[...]).astype(BF)

    pltpu.make_async_remote_copy(
        src_ref=cbuf.at[pl.ds(64, 192)], dst_ref=cbuf.at[pl.ds(64, 192)], send_sem=a_send, recv_sem=a_recv,
        device_id=first[0], device_id_type=MESH,
    ).wait()

    def ring(start, land, count, k, peer):
        return pltpu.make_async_remote_copy(
            src_ref=cbuf.at[pl.ds(start, count)], dst_ref=cbuf.at[pl.ds(land, count)],
            send_sem=b_send, recv_sem=b_recv.at[k], device_id=peer, device_id_type=MESH,
        )

    def block(k):
        return pl.ds(k * 256 if isinstance(k, int) else pl.multiple_of(k * 256, 256), 256)

    def swap(k):
        return pltpu.make_async_remote_copy(
            src_ref=cbuf.at[block(k)], dst_ref=cbuf.at[block(k + 4)],
            send_sem=c_send, recv_sem=c_recv.at[k], device_id=partner, device_id_type=MESH,
        )

    ring(0, 256, 256, 1, then[0]).start()
    ring(0, 512, 256, 2, then[1]).start()
    swap(0).start()

    for i in range(4):
        rows = slice(i * 352, i * 352 + 352)
        a = abuf[rows, :]
        kbuf[rows, :] = dot(a, wk_ref[...]).astype(BF)
        vbuf[rows, :] = dot(a, wv_ref[...]).astype(BF)

    lane_quad = lax.broadcasted_iota(jnp.int32, (1, 128), 1) // 32
    blank_f, blank_m = jnp.zeros((160, 128), BF), jnp.zeros((96, 128), BF)
    tally = jnp.concatenate(
        [
            jnp.concatenate([jnp.ones((160, 128), BF), blank_m], axis=0),
            jnp.concatenate([blank_f, jnp.ones((96, 128), BF)], axis=0),
        ],
        axis=1,
    )

    def windows(bx, carry):
        mx = lax.div(bx, 2)

        def rows(start, count):
            return pl.ds(pl.multiple_of(start, 16), count)

        def places(by):
            my = by // 2
            parts = [rows((2 * bx + i) * 80 + by * 16, 32) for i in range(4)] + [
                rows(AT_Z + by * 80 + bx * 16, 32),
                rows(AT_M + my * 96 + mx * 32, 64),
                rows(AT_MZ + my * 48 + mx * 16, 32),
            ]
            return rows(bx * 128 + by * 16, 16), rows(bx * 128 + by * 16 + 64, 16), parts

        def begin(unit):
            r0, r1, parts = places(unit // 2)
            lanes = slice(unit % 2 * 128, unit % 2 * 128 + 128)
            q = jnp.concatenate([qn[r0, lanes], qn[r1, lanes]], axis=0)
            heads = jnp.concatenate([jnp.where(lane_quad == h, q, jnp.zeros_like(q)) for h in range(4)], axis=0)
            keys = jnp.concatenate([kbuf[p, lanes] for p in parts], axis=0)
            wbuf[unit] = dot_t(heads, keys)

        def end(unit):
            r0, r1, parts = places(unit // 2)
            lanes = slice(unit % 2 * 128, unit % 2 * 128 + 128)
            fine = jnp.concatenate([vbuf[p, lanes] for p in parts[:5]] + [blank_m], axis=0)
            mids = jnp.concatenate([blank_f] + [vbuf[p, lanes] for p in parts[5:]], axis=0)
            left = wbuf[unit, :, 0:128].reshape(16, 8, 128)
            right = wbuf[unit, :, 128:256].reshape(16, 8, 128)
            s0 = (left + mask_ref[:, 0:128][None]).reshape(128, 128)
            sf = (right + mask_ref[:, 128:256][None]).reshape(128, 128)
            sm = (right + mask_ref[:, 256:384][None]).reshape(128, 128)
            top_f = jnp.max(jnp.maximum(s0, sf), axis=1, keepdims=True)
            top_m = jnp.max(sm, axis=1, keepdims=True)
            e = jnp.concatenate(
                [jnp.exp2(s0 - top_f), jnp.exp2(jnp.maximum(sf - top_f, sm - top_m))], axis=1
            ).astype(BF)
            mixed = dot(e, jnp.concatenate([fine, mids], axis=1)) / dot(e, tally)
            mixed = mixed[:, :128] + mixed[:, 128:]
            total = mixed[0:32, :]
            for h in range(1, 4):
                total = jnp.where(lane_quad == h, mixed[h * 32 : h * 32 + 32, :], total)
            fm[r0, lanes] = total[:16]
            fm[r1, lanes] = total[16:]

        for unit in range(AHEAD):
            begin(unit)
        for unit in range(8):
            if unit + AHEAD < 8:
                begin(unit + AHEAD)
            end(unit)
        return carry

    lax.fori_loop(0, 4, windows, 0)

    ring(256, 256, 256, 1, then[0]).wait_recv()
    ring(256, 768, 128, 3, then[0]).start()
    ring(512, 512, 256, 2, then[1]).wait_recv()
    ring(640, 896, 128, 3, then[1]).start()
    swap(1).start()
    swap(2).start()

    def scores_of(h):
        s = dot(kc[h // 4], qm[h])
        held[h] = s
        return jnp.max(s.reshape(32, 8, 512), axis=0)

    def absorb(h, block_top):
        old = ms[h]
        top = jnp.maximum(old, jnp.max(block_top, axis=0, keepdims=True))
        p = jnp.exp2(held[h] - top).astype(BF)
        acc[h] = acc[h] * jnp.exp2(old - top) + dot(va[h], p)
        ms[h] = top

    def coarse_block(j, carry):
        s, other = lax.div(j, 2), lax.rem(j, 2)

        @pl.when(j == 3)
        def _():
            ring(768, 768, 256, 3, then[0]).wait_recv()
            swap(3).start()

        @pl.when(other == 1)
        def _():
            swap(s).wait_recv()

        c = cbuf[pl.ds(pl.multiple_of(1024 * other + 256 * s, 256), 256), :]
        k = dot(c, wk_ref[...]).astype(BF)
        kc[0] = k[:, :128]
        kc[1] = k[:, 128:]
        v = dot_t(wvt[...], c).astype(BF)
        for h in range(HEADS):
            va[h, 0:32, :] = v[h * 32 : h * 32 + 32, :]
        tops = [scores_of(h) for h in range(3)]
        for h in range(HEADS):
            if h + 3 < HEADS:
                tops.append(scores_of(h + 3))
            absorb(h, tops[h])
        return carry

    lax.fori_loop(0, 8, coarse_block, 0)

    for load in loads[1:]:
        load.wait()
    turned_out = jnp.concatenate([acc[h, 0:32, :] / acc[h, 32:33, :] for h in range(HEADS)], axis=0)
    fm[...] = fm[...] + turned_out.T

    for i in range(4):
        rows = slice(i * 128, i * 128 + 128)
        attended = fm[rows, :].astype(BF)
        residual = (tok_ref[rows, :].astype(F32) + dot(attended, wo_ref[...])).astype(BF)
        wide = residual.astype(F32)
        second = normalized(wide, gain2_ref[...])
        hidden = jax.nn.gelu(dot(second, up_ref[...]), approximate=True).astype(BF)
        out_ref[rows, :] = (wide + dot(hidden, down_ref[...])).astype(BF)

    pltpu.make_async_remote_copy(
        src_ref=cbuf.at[pl.ds(256, 768)], dst_ref=cbuf.at[pl.ds(256, 768)], send_sem=b_send, recv_sem=b_recv.at[0],
        device_id=then[0], device_id_type=MESH,
    ).wait_send()
    pltpu.make_async_remote_copy(
        src_ref=cbuf.at[pl.ds(0, 1024)], dst_ref=cbuf.at[pl.ds(0, 1024)], send_sem=c_send, recv_sem=c_recv.at[0],
        device_id=partner, device_id_type=MESH,
    ).wait_send()


def shards(
    tokens, norm_gain, query_weight, key_weight, value_weight, head_scale, out_weight, mlp_gain, up_weight, down_weight
):
    shape = tokens.shape
    vmem = pl.BlockSpec(memory_space=pltpu.VMEM)
    smem = pl.BlockSpec(memory_space=pltpu.SMEM)
    hbm = pl.BlockSpec(memory_space=pl.ANY)
    dma = pltpu.SemaphoreType.DMA
    V = pltpu.VMEM
    flat = pl.pallas_call(
        layer_kernel,
        out_shape=jax.ShapeDtypeStruct((512, 256), BF),
        in_specs=[vmem, vmem, vmem, vmem, vmem, smem, hbm, vmem, hbm, hbm, hbm, vmem],
        out_specs=vmem,
        scratch_shapes=[
            V((2, 512, 128), F32),
            V((2, 64, 128), F32),
            V((2, 128, 128), F32),
            V((2, 32, 128), F32),
            V((2, PACKED, 128), F32),
            V((PACKED, 256), BF),
            V((SRC, 256), BF),
            V((8, 8, 256), BF),
            V((2048, 256), BF),
            V((KEYS, 256), BF),
            V((512, 256), BF),
            V((8, 128, 512), BF),
            V((KEYS, 256), BF),
            V((KEYS, 256), BF),
            V((8, 128, 256), F32),
            V((512, 256), F32),
            V((2, 256, 128), BF),
            V((8, 48, 256), BF),
            V((8, 256, 512), F32),
            V((8, 1, 512), F32),
            V((8, 48, 512), F32),
            V((256, 256), BF),
            V((256, 512), BF),
            V((512, 256), BF),
            V((KEYS - AT_Z, SRC), BF),
            V((256, 256), BF),
            dma((4,)),
            dma,
            dma,
            dma,
            dma,
            dma,
            dma,
            dma,
            dma((4,)),
            dma,
            dma((4,)),
        ],
        compiler_params=pltpu.CompilerParams(
            collective_id=0, has_side_effects=True, vmem_limit_bytes=60 << 20
        ),
        name="layer",
    )(
        tokens.reshape(512, 256),
        norm_gain.reshape(1, 256),
        query_weight,
        key_weight,
        value_weight,
        head_scale,
        out_weight,
        mlp_gain.reshape(1, 256),
        up_weight,
        down_weight,
        jnp.asarray(selection(), BF),
        jnp.asarray(window_masks()),
    )
    return flat.reshape(shape)


def solution(mesh):
    in_specs = (P("gx", "gy", "gz", None), P(), P(), P(), P(), P(), P(), P(), P(), P())
    step = jax.shard_map(shards, mesh=mesh, in_specs=in_specs, out_specs=P("gx", "gy", "gz", None), check_vma=False)

    def traced(*arguments):
        with jax.sharding.use_abstract_mesh(mesh.abstract_mesh):
            return step(*arguments)

    return traced
```

```python
import functools
import math

import jax
import jax.numpy as jnp
import numpy as np
from jax import lax
from jax.experimental import pallas as pl
from jax.experimental.pallas import tpu as pltpu
from jax.sharding import PartitionSpec as P

MESH = pl.DeviceIdType.MESH
BF = jnp.bfloat16
F32 = jnp.float32
HEADS = 8
EPSILON = 1e-05
LOG2E = math.log2(math.e)
NEG = -1e30
AHEAD = 3

FACES = [(1, 0, 0), (-1, 0, 0), (0, 1, 0), (0, -1, 0), (0, 0, 1), (0, 0, -1)]
OTHERS = [
    (i, j, k)
    for i in (1, 0, -1)
    for j in (1, 0, -1)
    for k in (1, 0, -1)
    if abs(i) + abs(j) + abs(k) > 1
]
DIRS = FACES + OTHERS
PACKED = 800
SRC = 1024
MID_AT = 896


def slot(d):
    if d in FACES:
        return 80 * FACES.index(d), 80
    return 512 + 16 * OTHERS.index(d), 16


def packed_slot(d):
    start, rows = slot(d)
    return (start if start < 512 else start - 32), rows


AT_Z, AT_M, AT_MZ, KEYS = 800, 1120, 1312, 1408


def halo_row(x, y, z, n, middle):
    d = tuple(1 if c == 0 else -1 if c == n + 1 else 0 for c in (x, y, z))
    free = [c - 1 for c, e in zip((x, y, z), d) if e == 0]
    if not any(d):
        return MID_AT + (free[0] * n + free[1]) * n + free[2]
    start, rows = slot(d)
    at = 0
    for c in free:
        at = at * n + c
    return start + at + ((64 if rows == 80 else 8) if middle else 0)


def selection():
    pick = np.zeros((KEYS - AT_Z, SRC), np.float32)
    for by in range(4):
        for x in range(10):
            for yy in range(4):
                for s in range(2):
                    row = by * 80 + x * 8 + yy * 2 + s
                    pick[row, halo_row(x, 2 * by + yy, 9 * s, 8, False)] = 1
    for my in range(2):
        for x in range(6):
            for yy in range(4):
                for z in range(4):
                    row = AT_M - AT_Z + my * 96 + x * 16 + yy * 4 + z
                    pick[row, halo_row(x, 2 * my + yy, z + 1, 4, True)] = 1
                for s in range(2):
                    row = AT_MZ - AT_Z + my * 48 + x * 8 + yy * 2 + s
                    pick[row, halo_row(x, 2 * my + yy, 5 * s, 4, True)] = 1
    return pick


def window_masks():
    mask = np.full((8, 384), NEG, np.float32)
    for q in range(8):
        for lane in range(256):
            if lane < 128:
                at, low, put = lane % 8 + 1, 2 * (q // 2), lane
            elif lane < 160:
                at, low, put = 9 * (lane % 2), 2 * (q // 2), lane
            elif lane < 224:
                at, low, put = lane % 4 + 1, 2 * (q // 4), lane + 128
            else:
                at, low, put = 5 * (lane % 2), 2 * (q // 4), lane + 128
            if low <= at <= low + 3:
                mask[q, put] = 0
    return mask


def dot(a, b):
    return jnp.dot(a, b, preferred_element_type=F32)


def dot_t(a, b):
    return lax.dot_general(a, b, (((1,), (1,)), ((), ())), preferred_element_type=F32)


def normalized(values, gain):
    average = jnp.mean(values, axis=-1, keepdims=True)
    centered = values - average
    variance = jnp.mean(centered * centered, axis=-1, keepdims=True)
    return (centered * lax.rsqrt(variance + EPSILON) * gain).astype(BF)


def cf_rows(cf, k):
    return jnp.concatenate([cf[c, pl.ds(k, 8, stride=4), :] for c in range(2)], axis=1)


def layer_kernel(
    tok_hbm, gain_hbm, wq_hbm, wk_hbm, wv_hbm, scale_hbm, pick_hbm, mask_hbm,
    out_ref,
    nf, mf, tf, cf, stage, packed, src, zbuf, cbuf, abuf, qn, qm, kbuf, vbuf, wbuf, fm, kc, va, held, ms, acc,
    tok_ref, gain_ref, wq_ref, wk_ref, wv_ref, scale_ref, pick_ref, mask_ref, wvt,
    load_sem, halo_send, halo_recv, z_send, z_recv, a_send, a_recv, b_send, b_recv, c_send, c_recv,
):
    loads = [
        pltpu.make_async_copy(a, b, load_sem.at[i])
        for i, (a, b) in enumerate(
            (
                (tok_hbm, tok_ref), (gain_hbm, gain_ref), (scale_hbm, scale_ref), (wq_hbm, wq_ref), (wv_hbm, wv_ref),
                (wk_hbm, wk_ref), (pick_hbm, pick_ref), (mask_hbm, mask_ref),
            )
        )
    ]
    for load in loads:
        load.start()

    gx, gy, gz = lax.axis_index("gx"), lax.axis_index("gy"), lax.axis_index("gz")
    core, ylow = lax.rem(gx, 2), lax.div(gx, 2)
    xpos, yhigh = lax.div(gy, 2), lax.rem(gy, 2)
    ypos = yhigh * 2 + ylow

    def chip(x, y):
        return (lax.rem(y, 2) * 2 + core, x * 2 + lax.div(y, 2), gz)

    near = [
        (lax.rem(gx + d[0] + 4, 4), lax.rem(gy + d[1] + 8, 8), lax.rem(gz + d[2] + 8, 8))
        for d in DIRS
    ]
    along_z = [(gx, gy, lax.rem(gz + k, 8)) for k in range(1, 8)]
    first = [chip(lax.rem(xpos + k * (1 - core), 4), lax.rem(ypos + k * core, 4)) for k in range(1, 4)]
    then = [chip(lax.rem(xpos + k * core, 4), lax.rem(ypos + k * (1 - core), 4)) for k in (1, 3)]
    partner = (gx + 1 - 2 * core, gy, gz)

    barrier = pltpu.get_barrier_semaphore()
    greeted = along_z[1:6] + near[::-1] + first + then
    for peer in greeted:
        pl.semaphore_signal(barrier, inc=1, device_id=peer, device_id_type=MESH)

    loads[0].wait()
    loads[1].wait()
    normed = normalized(tok_ref[...].astype(F32), gain_ref[...])
    widened = normed.astype(F32)
    for c in range(2):
        half = widened[:, c * 128 : c * 128 + 128]
        nf[c] = half
        pairs = jnp.sum(half.reshape(4, 2, 4, 2, 8, 128), axis=(1, 3))
        tf[c] = pairs.reshape(128, 128)
        mf[c] = ((tf[c, pl.ds(0, 64, stride=2), :] + tf[c, pl.ds(1, 64, stride=2), :]) * 0.125).astype(BF).astype(F32)
        cf[c] = jnp.sum(pairs.reshape(2, 2, 2, 2, 8, 128), axis=(1, 3)).reshape(32, 128)
    coarse = cf_rows(cf, 0)
    for k in range(1, 4):
        coarse = coarse + cf_rows(cf, k)
    zbuf[0] = (coarse * (1.0 / 64)).astype(BF)

    for d in DIRS:
        start, rows = packed_slot(d)
        x, y, z = (7 if c > 0 else 0 for c in d)
        mx, my, mz = (3 if c > 0 else 0 for c in d)
        axes = tuple(c != 0 for c in d)
        at = start + (64 if rows == 80 else 8)
        for c in range(2):
            if rows == 16:
                stage[c, start : start + 16, :] = jnp.zeros((16, 128), F32)
            if axes == (True, False, False):
                stage[c, start : start + 64, :] = nf[c, x * 64 : x * 64 + 64, :]
                stage[c, at : at + 16, :] = mf[c, mx * 16 : mx * 16 + 16, :]
            elif axes == (False, True, False):
                for i in range(8):
                    stage[c, start + i * 8 : start + i * 8 + 8, :] = nf[c, i * 64 + y * 8 : i * 64 + y * 8 + 8, :]
                for i in range(4):
                    stage[c, at + i * 4 : at + i * 4 + 4, :] = mf[c, i * 16 + my * 4 : i * 16 + my * 4 + 4, :]
            elif axes == (False, False, True):
                stage[c, start : start + 64, :] = nf[c, pl.ds(z, 64, stride=8), :]
                stage[c, at : at + 16, :] = mf[c, pl.ds(mz, 16, stride=4), :]
            elif axes == (True, True, False):
                stage[c, start : start + 8, :] = nf[c, x * 64 + y * 8 : x * 64 + y * 8 + 8, :]
                stage[c, at : at + 4, :] = mf[c, mx * 16 + my * 4 : mx * 16 + my * 4 + 4, :]
            elif axes == (True, False, True):
                stage[c, start : start + 8, :] = nf[c, pl.ds(x * 64 + z, 8, stride=8), :]
                stage[c, at : at + 4, :] = mf[c, pl.ds(mx * 16 + mz, 4, stride=4), :]
            elif axes == (False, True, True):
                stage[c, start : start + 8, :] = nf[c, pl.ds(y * 8 + z, 8, stride=64), :]
                stage[c, at : at + 4, :] = mf[c, pl.ds(my * 4 + mz, 4, stride=16), :]
            else:
                row, mrow = x * 64 + y * 8 + z, mx * 16 + my * 4 + mz
                stage[c, start : start + 1, :] = nf[c, row : row + 1, :]
                stage[c, at : at + 1, :] = mf[c, mrow : mrow + 1, :]
    packed[...] = jnp.concatenate([stage[0], stage[1]], axis=1).astype(BF)

    src[480:512, :] = jnp.zeros((32, 256), BF)
    src[832:896, :] = jnp.zeros((64, 256), BF)
    src[960:1024, :] = jnp.zeros((64, 256), BF)
    src[MID_AT : MID_AT + 64, :] = jnp.concatenate([mf[0], mf[1]], axis=1).astype(BF)

    pl.semaphore_wait(barrier, len(greeted))

    z_copies = [
        pltpu.make_async_remote_copy(
            src_ref=zbuf.at[0], dst_ref=zbuf.at[k], send_sem=z_send, recv_sem=z_recv,
            device_id=along_z[k - 1], device_id_type=MESH,
        )
        for k in range(1, 8)
    ]
    for copy in z_copies:
        copy.start()
    halo = []
    for i, d in enumerate(DIRS):
        start, rows = packed_slot(d)
        land, _ = slot(d)
        halo.append(
            pltpu.make_async_remote_copy(
                src_ref=packed.at[pl.ds(start, rows)], dst_ref=src.at[pl.ds(land, rows)],
                send_sem=halo_send, recv_sem=halo_recv, device_id=near[i], device_id_type=MESH,
            )
        )
    for copy in halo:
        copy.start()

    for load in loads[2:5]:
        load.wait()
    factor = LOG2E / math.sqrt(32)
    lane_head = lax.broadcasted_iota(jnp.int32, (1, 256), 1) // 32
    spread = jnp.zeros((1, 256), F32)
    for h in range(HEADS):
        spread = jnp.where(lane_head == h, scale_ref[h] * factor, spread)
    qn[...] = (dot(normed, wq_ref[...]) * spread).astype(BF)
    turned = dot_t(wq_ref[...].T, normed)
    qm[...] = jnp.zeros_like(qm)
    for h in range(HEADS):
        at = (h % 4) * 32
        qm[h, at : at + 32, :] = (turned[h * 32 : h * 32 + 32, :] * (scale_ref[h] * factor)).astype(BF)
    wvt[...] = wv_ref[...].T
    for part in range(2):
        va[part, :, 32:48, :] = jnp.ones((HEADS, 16, 256), BF)
    ms[...] = jnp.full_like(ms, NEG)
    acc[...] = jnp.zeros_like(acc)

    pltpu.make_async_remote_copy(
        src_ref=zbuf.at[pl.ds(1, 7)], dst_ref=zbuf.at[pl.ds(1, 7)], send_sem=z_send, recv_sem=z_recv,
        device_id=along_z[0], device_id_type=MESH,
    ).wait()
    cbuf[0:64, :] = zbuf[...].astype(F32).reshape(64, 256).astype(BF)
    a_copies = [
        pltpu.make_async_remote_copy(
            src_ref=cbuf.at[pl.ds(0, 64)], dst_ref=cbuf.at[pl.ds(64 * k, 64)],
            send_sem=a_send, recv_sem=a_recv, device_id=first[k - 1], device_id_type=MESH,
        )
        for k in range(1, 4)
    ]
    for copy in a_copies:
        copy.start()

    pltpu.make_async_remote_copy(
        src_ref=packed, dst_ref=packed, send_sem=halo_send, recv_sem=halo_recv,
        device_id=near[0], device_id_type=MESH,
    ).wait()

    def cells(d, row):
        start, _ = slot(d)
        at = start + row
        low = at - at % 16
        tile = src[low : low + 16, :].astype(F32)
        return tile[at - low : at - low + 8, :]

    for x in range(10):
        ex = 1 if x == 0 else -1 if x == 9 else 0
        if ex:
            begin, end = cells((ex, 1, 0), 0), cells((ex, -1, 0), 0)
            start, _ = slot((ex, 0, 0))
            inner = src[start : start + 64, :].astype(F32)
        else:
            begin, end = cells((0, 1, 0), (x - 1) * 8), cells((0, -1, 0), (x - 1) * 8)
            own = slice((x - 1) * 64, x * 64)
            inner = jnp.concatenate([nf[0, own, :], nf[1, own, :]], axis=1)
        abuf[x * 80 : x * 80 + 80, :] = jnp.concatenate([begin, inner, end], axis=0).astype(BF)
    for load in loads[5:]:
        load.wait()
    abuf[AT_Z:KEYS, :] = dot(pick_ref[...], src[...]).astype(BF)

    pltpu.make_async_remote_copy(
        src_ref=cbuf.at[pl.ds(64, 192)], dst_ref=cbuf.at[pl.ds(64, 192)], send_sem=a_send, recv_sem=a_recv,
        device_id=first[0], device_id_type=MESH,
    ).wait()

    def ring(start, land, count, k, peer):
        return pltpu.make_async_remote_copy(
            src_ref=cbuf.at[pl.ds(start, count)], dst_ref=cbuf.at[pl.ds(land, count)],
            send_sem=b_send, recv_sem=b_recv.at[k], device_id=peer, device_id_type=MESH,
        )

    def block(k):
        return pl.ds(k * 256 if isinstance(k, int) else pl.multiple_of(k * 256, 256), 256)

    def swap(k):
        return pltpu.make_async_remote_copy(
            src_ref=cbuf.at[block(k)], dst_ref=cbuf.at[block(k + 4)],
            send_sem=c_send, recv_sem=c_recv.at[k], device_id=partner, device_id_type=MESH,
        )

    ring(0, 256, 256, 1, then[0]).start()
    ring(0, 512, 256, 2, then[1]).start()
    swap(0).start()

    for i in range(4):
        rows = slice(i * 352, i * 352 + 352)
        a = abuf[rows, :]
        kbuf[rows, :] = dot(a, wk_ref[...]).astype(BF)
        vbuf[rows, :] = dot(a, wv_ref[...]).astype(BF)

    lane_quad = lax.broadcasted_iota(jnp.int32, (1, 128), 1) // 32
    blank_f, blank_m = jnp.zeros((160, 128), BF), jnp.zeros((96, 128), BF)
    tally = jnp.concatenate(
        [
            jnp.concatenate([jnp.ones((160, 128), BF), blank_m], axis=0),
            jnp.concatenate([blank_f, jnp.ones((96, 128), BF)], axis=0),
        ],
        axis=1,
    )

    def windows(bx, carry):
        mx = lax.div(bx, 2)

        def rows(start, count):
            return pl.ds(pl.multiple_of(start, 16), count)

        def places(by):
            my = by // 2
            parts = [rows((2 * bx + i) * 80 + by * 16, 32) for i in range(4)] + [
                rows(AT_Z + by * 80 + bx * 16, 32),
                rows(AT_M + my * 96 + mx * 32, 64),
                rows(AT_MZ + my * 48 + mx * 16, 32),
            ]
            return rows(bx * 128 + by * 16, 16), rows(bx * 128 + by * 16 + 64, 16), parts

        def begin(unit):
            r0, r1, parts = places(unit // 2)
            lanes = slice(unit % 2 * 128, unit % 2 * 128 + 128)
            q = jnp.concatenate([qn[r0, lanes], qn[r1, lanes]], axis=0)
            heads = jnp.concatenate([jnp.where(lane_quad == h, q, jnp.zeros_like(q)) for h in range(4)], axis=0)
            keys = jnp.concatenate([kbuf[p, lanes] for p in parts], axis=0)
            wbuf[unit] = dot_t(heads, keys)

        def end(unit):
            r0, r1, parts = places(unit // 2)
            lanes = slice(unit % 2 * 128, unit % 2 * 128 + 128)
            fine = jnp.concatenate([vbuf[p, lanes] for p in parts[:5]] + [blank_m], axis=0)
            mids = jnp.concatenate([blank_f] + [vbuf[p, lanes] for p in parts[5:]], axis=0)
            left = wbuf[unit, :, 0:128].reshape(16, 8, 128)
            right = wbuf[unit, :, 128:256].reshape(16, 8, 128)
            s0 = (left + mask_ref[:, 0:128][None]).reshape(128, 128)
            sf = (right + mask_ref[:, 128:256][None]).reshape(128, 128)
            sm = (right + mask_ref[:, 256:384][None]).reshape(128, 128)
            top_f = jnp.max(jnp.maximum(s0, sf), axis=1, keepdims=True)
            top_m = jnp.max(sm, axis=1, keepdims=True)
            e = jnp.concatenate(
                [jnp.exp2(s0 - top_f), jnp.exp2(jnp.maximum(sf - top_f, sm - top_m))], axis=1
            ).astype(BF)
            mixed = dot(e, jnp.concatenate([fine, mids], axis=1)) / dot(e, tally)
            mixed = mixed[:, :128] + mixed[:, 128:]
            total = mixed[0:32, :]
            for h in range(1, 4):
                total = jnp.where(lane_quad == h, mixed[h * 32 : h * 32 + 32, :], total)
            fm[r0, lanes] = total[:16]
            fm[r1, lanes] = total[16:]

        for unit in range(AHEAD):
            begin(unit)
        for unit in range(8):
            if unit + AHEAD < 8:
                begin(unit + AHEAD)
            end(unit)
        return carry

    lax.fori_loop(0, 4, windows, 0)

    ring(256, 256, 256, 1, then[0]).wait_recv()
    ring(256, 768, 128, 3, then[0]).start()
    ring(512, 512, 256, 2, then[1]).wait_recv()
    ring(640, 896, 128, 3, then[1]).start()
    swap(1).start()
    swap(2).start()

    def scores_of(unit):
        part, h = unit // HEADS, unit % HEADS
        s = dot(kc[part, h // 4], qm[h])
        held[unit] = s
        return jnp.max(s.reshape(32, 8, 512), axis=0)

    def absorb(unit, block_top):
        part, h = unit // HEADS, unit % HEADS
        old = ms[h]
        top = jnp.maximum(old, jnp.max(block_top, axis=0, keepdims=True))
        p = jnp.exp2(held[unit] - top).astype(BF)
        acc[h] = acc[h] * jnp.exp2(old - top) + dot(va[part, h], p)
        ms[h] = top

    def coarse_block(j, carry):
        @pl.when(j == 1)
        def _():
            ring(768, 768, 256, 3, then[0]).wait_recv()
            swap(3).start()

        swap(j).wait_recv()

        def project_keys(part):
            k = dot(cbuf[block(j + 4 * part), :], wk_ref[...]).astype(BF)
            kc[part, 0] = k[:, :128]
            kc[part, 1] = k[:, 128:]

        def project_values(part):
            v = dot_t(wvt[...], cbuf[block(j + 4 * part), :]).astype(BF)
            for h in range(HEADS):
                va[part, h, 0:32, :] = v[h * 32 : h * 32 + 32, :]

        project_keys(0)
        tops = [scores_of(h) for h in range(3)]
        project_values(0)
        for unit in range(2 * HEADS):
            if unit == 2:
                project_keys(1)
            if unit == 4:
                project_values(1)
            if unit + 3 < 2 * HEADS:
                tops.append(scores_of(unit + 3))
            absorb(unit, tops[unit])
        return carry

    lax.fori_loop(0, 4, coarse_block, 0)

    turned_out = jnp.concatenate([acc[h, 0:32, :] / acc[h, 32:33, :] for h in range(HEADS)], axis=0)
    out_ref[...] = (fm[...] + turned_out.T).astype(BF)

    pltpu.make_async_remote_copy(
        src_ref=cbuf.at[pl.ds(256, 768)], dst_ref=cbuf.at[pl.ds(256, 768)], send_sem=b_send, recv_sem=b_recv.at[0],
        device_id=then[0], device_id_type=MESH,
    ).wait_send()
    pltpu.make_async_remote_copy(
        src_ref=cbuf.at[pl.ds(0, 1024)], dst_ref=cbuf.at[pl.ds(0, 1024)], send_sem=c_send, recv_sem=c_recv.at[0],
        device_id=partner, device_id_type=MESH,
    ).wait_send()


def finish_kernel(att_ref, tok_ref, wo_ref, gain2_ref, up_ref, down_ref, out_ref):
    for i in range(4):
        rows = slice(i * 128, i * 128 + 128)
        residual = (tok_ref[rows, :].astype(F32) + dot(att_ref[rows, :], wo_ref[...])).astype(BF)
        wide = residual.astype(F32)
        second = normalized(wide, gain2_ref[...])
        hidden = jax.nn.gelu(dot(second, up_ref[...]), approximate=True).astype(BF)
        out_ref[rows, :] = (wide + dot(hidden, down_ref[...])).astype(BF)


def shards(
    tokens, norm_gain, query_weight, key_weight, value_weight, head_scale, out_weight, mlp_gain, up_weight, down_weight
):
    shape = tokens.shape
    vmem = pl.BlockSpec(memory_space=pltpu.VMEM)
    hbm = pl.BlockSpec(memory_space=pltpu.MemorySpace.HBM)
    dma = pltpu.SemaphoreType.DMA
    V = pltpu.VMEM
    flat_tokens = tokens.reshape(512, 256)
    attended = pl.pallas_call(
        layer_kernel,
        out_shape=jax.ShapeDtypeStruct((512, 256), BF),
        in_specs=[hbm] * 8,
        out_specs=vmem,
        scratch_shapes=[
            V((2, 512, 128), F32),
            V((2, 64, 128), F32),
            V((2, 128, 128), F32),
            V((2, 32, 128), F32),
            V((2, PACKED, 128), F32),
            V((PACKED, 256), BF),
            V((SRC, 256), BF),
            V((8, 8, 256), BF),
            V((2048, 256), BF),
            V((KEYS, 256), BF),
            V((512, 256), BF),
            V((8, 128, 512), BF),
            V((KEYS, 256), BF),
            V((KEYS, 256), BF),
            V((8, 128, 256), F32),
            V((512, 256), F32),
            V((2, 2, 256, 128), BF),
            V((2, 8, 48, 256), BF),
            V((16, 256, 512), F32),
            V((8, 1, 512), F32),
            V((8, 48, 512), F32),
            V((512, 256), BF),
            V((1, 256), F32),
            V((256, 256), BF),
            V((256, 256), BF),
            V((256, 256), BF),
            pltpu.SMEM((8,), F32),
            V((KEYS - AT_Z, SRC), BF),
            V((8, 384), F32),
            V((256, 256), BF),
            dma((8,)),
            dma,
            dma,
            dma,
            dma,
            dma,
            dma,
            dma,
            dma((4,)),
            dma,
            dma((4,)),
        ],
        compiler_params=pltpu.CompilerParams(
            collective_id=0, has_side_effects=True, vmem_limit_bytes=28 << 20
        ),
        name="layer",
    )(
        *(
            pltpu.with_memory_space_constraint(a, pltpu.MemorySpace.HBM)
            for a in (
                flat_tokens,
                norm_gain.reshape(1, 256),
                query_weight,
                key_weight,
                value_weight,
                head_scale,
                jnp.asarray(selection(), BF),
                jnp.asarray(window_masks()),
            )
        )
    )
    flat = pl.pallas_call(
        finish_kernel,
        out_shape=jax.ShapeDtypeStruct((512, 256), BF),
        in_specs=[vmem] * 6,
        out_specs=vmem,
        compiler_params=pltpu.CompilerParams(vmem_limit_bytes=12 << 20),
        name="finish",
    )(attended, flat_tokens, out_weight, mlp_gain.reshape(1, 256), up_weight, down_weight)
    return flat.reshape(shape)


def solution(mesh):
    in_specs = (P("gx", "gy", "gz", None), P(), P(), P(), P(), P(), P(), P(), P(), P())
    step = jax.shard_map(shards, mesh=mesh, in_specs=in_specs, out_specs=P("gx", "gy", "gz", None), check_vma=False)

    def traced(*arguments):
        with jax.sharding.use_abstract_mesh(mesh.abstract_mesh):
            return step(*arguments)

    return traced
```

```python
import functools
import math

import jax
import jax.numpy as jnp
import numpy as np
from jax import lax
from jax.experimental import pallas as pl
from jax.experimental.pallas import tpu as pltpu
from jax.sharding import PartitionSpec as P

MESH = pl.DeviceIdType.MESH
BF = jnp.bfloat16
F32 = jnp.float32
HEADS = 8
EPSILON = 1e-05
LOG2E = math.log2(math.e)
GELU = math.sqrt(2 / math.pi)
NEG = -1e30
AHEAD = 3

SIGNS = (1, 0, -1)
ALL = [(i, j, k) for i in SIGNS for j in SIGNS for k in SIGNS if (i, j, k) != (0, 0, 0)]
ALL.sort(key=lambda d: sum(map(abs, d)))
NEAR = [d for d in ALL if d[1] == 0]
FAR = [d for d in ALL if d[1] != 0]
DIRS = FAR + NEAR
OWN_AT, SIBLING_AT = (0, 512, 768, 1536), (256, 1024, 1280, 1792)
SRC = 1024
MID_AT = 384
NEAR_ROWS, FAR_AT, FAR_ROWS = 384, 512, 416


def slot(d):
    group, at = (NEAR, 0) if d in NEAR else (FAR, FAR_AT)
    for other in group:
        rows = 80 if sum(map(abs, other)) == 1 else 16
        if other == d:
            return at, rows
        at += rows


AT_Z, AT_M, AT_MZ, KEYS = 800, 1120, 1312, 1408


def halo_row(x, y, z, n, middle):
    d = tuple(1 if c == 0 else -1 if c == n + 1 else 0 for c in (x, y, z))
    free = [c - 1 for c, e in zip((x, y, z), d) if e == 0]
    if not any(d):
        return MID_AT + (free[0] * n + free[1]) * n + free[2]
    start, rows = slot(d)
    at = 0
    for c in free:
        at = at * n + c
    return start + at + ((64 if rows == 80 else 8) if middle else 0)


def selection():
    pick = np.zeros((KEYS - AT_Z, SRC), np.float32)
    for by in range(4):
        for x in range(10):
            for yy in range(4):
                for s in range(2):
                    row = by * 80 + x * 8 + yy * 2 + s
                    pick[row, halo_row(x, 2 * by + yy, 9 * s, 8, False)] = 1
    for my in range(2):
        for x in range(6):
            for yy in range(4):
                for z in range(4):
                    row = AT_M - AT_Z + my * 96 + x * 16 + yy * 4 + z
                    pick[row, halo_row(x, 2 * my + yy, z + 1, 4, True)] = 1
                for s in range(2):
                    row = AT_MZ - AT_Z + my * 48 + x * 8 + yy * 2 + s
                    pick[row, halo_row(x, 2 * my + yy, 5 * s, 4, True)] = 1
    return pick


def window_masks():
    mask = np.full((8, 384), NEG, np.float32)
    for q in range(8):
        for lane in range(256):
            if lane < 128:
                at, low, put = lane % 8 + 1, 2 * (q // 2), lane
            elif lane < 160:
                at, low, put = 9 * (lane % 2), 2 * (q // 2), lane
            elif lane < 224:
                at, low, put = lane % 4 + 1, 2 * (q // 4), lane + 128
            else:
                at, low, put = 5 * (lane % 2), 2 * (q // 4), lane + 128
            if low <= at <= low + 3:
                mask[q, put] = 0
    return mask


def dot(a, b):
    return jnp.dot(a, b, preferred_element_type=F32)


def dot_t(a, b):
    return lax.dot_general(a, b, (((1,), (1,)), ((), ())), preferred_element_type=F32)


def normalized(values, gain):
    average = jnp.mean(values, axis=-1, keepdims=True)
    centered = values - average
    variance = jnp.mean(centered * centered, axis=-1, keepdims=True)
    return (centered * lax.rsqrt(variance + EPSILON) * gain).astype(BF)


def cf_rows(cf, k):
    return jnp.concatenate([cf[c, pl.ds(k, 8, stride=4), :] for c in range(2)], axis=1)


def layer_kernel(
    tok_hbm, gain_hbm, wq_hbm, wk_hbm, wv_hbm, scale_hbm, pick_hbm, mask_hbm,
    out_ref,
    nf, mf, tf, cf, stage, packed, src, zbuf, cbuf, abuf, qn, qm, kbuf, vbuf, wbuf, fm, kc, va, held, ms, acc,
    tok_ref, gain_ref, wq_ref, wk_ref, wv_ref, scale_ref, pick_ref, mask_ref, wvt, picked,
    load_sem, halo_send, halo_recv, far_send, far_recv, z_send, z_recv, a_send, a_recv, b_send, b_recv, c_send, c_recv,
):
    loads = [
        pltpu.make_async_copy(a, b, load_sem.at[i])
        for i, (a, b) in enumerate(
            (
                (tok_hbm, tok_ref), (gain_hbm, gain_ref), (scale_hbm, scale_ref), (wq_hbm, wq_ref), (wv_hbm, wv_ref),
                (wk_hbm, wk_ref), (pick_hbm, pick_ref), (mask_hbm, mask_ref),
            )
        )
    ]
    for load in loads:
        load.start()

    gx, gy, gz = lax.axis_index("gx"), lax.axis_index("gy"), lax.axis_index("gz")
    core, ylow = lax.rem(gx, 2), lax.div(gx, 2)
    xpos, yhigh = lax.div(gy, 2), lax.rem(gy, 2)
    ypos = yhigh * 2 + ylow

    def chip(x, y):
        return (lax.rem(y, 2) * 2 + core, x * 2 + lax.div(y, 2), gz)

    near = [
        (lax.rem(gx + d[0] + 4, 4), lax.rem(gy + d[1] + 8, 8), lax.rem(gz + d[2] + 8, 8))
        for d in DIRS
    ]
    along_z = [(gx, gy, lax.rem(gz + k, 8)) for k in range(1, 8)]
    first = [chip(lax.rem(xpos + k * (1 - core), 4), lax.rem(ypos + k * core, 4)) for k in range(1, 4)]
    then = [chip(lax.rem(xpos + k * core, 4), lax.rem(ypos + k * (1 - core), 4)) for k in (1, 3)]
    partner = (gx + 1 - 2 * core, gy, gz)

    barrier = pltpu.get_barrier_semaphore()
    greeted = along_z[1:6] + near[::-1] + first + then
    for peer in greeted:
        pl.semaphore_signal(barrier, inc=1, device_id=peer, device_id_type=MESH)

    loads[0].wait()
    loads[1].wait()
    normed = normalized(tok_ref[...].astype(F32), gain_ref[...])
    widened = normed.astype(F32)
    for c in range(2):
        half = widened[:, c * 128 : c * 128 + 128]
        nf[c] = half
        pairs = jnp.sum(half.reshape(4, 2, 4, 2, 8, 128), axis=(1, 3))
        tf[c] = pairs.reshape(128, 128)
        mf[c] = ((tf[c, pl.ds(0, 64, stride=2), :] + tf[c, pl.ds(1, 64, stride=2), :]) * 0.125).astype(BF).astype(F32)
        cf[c] = jnp.sum(pairs.reshape(2, 2, 2, 2, 8, 128), axis=(1, 3)).reshape(32, 128)
    coarse = cf_rows(cf, 0)
    for k in range(1, 4):
        coarse = coarse + cf_rows(cf, k)
    zbuf[0] = (coarse * (1.0 / 64)).astype(BF)

    for d in DIRS:
        start, rows = slot(d)
        x, y, z = (7 if c > 0 else 0 for c in d)
        mx, my, mz = (3 if c > 0 else 0 for c in d)
        axes = tuple(c != 0 for c in d)
        at = start + (64 if rows == 80 else 8)
        for c in range(2):
            if rows == 16:
                stage[c, start : start + 16, :] = jnp.zeros((16, 128), F32)
            if axes == (True, False, False):
                stage[c, start : start + 64, :] = nf[c, x * 64 : x * 64 + 64, :]
                stage[c, at : at + 16, :] = mf[c, mx * 16 : mx * 16 + 16, :]
            elif axes == (False, True, False):
                for i in range(8):
                    stage[c, start + i * 8 : start + i * 8 + 8, :] = nf[c, i * 64 + y * 8 : i * 64 + y * 8 + 8, :]
                for i in range(4):
                    stage[c, at + i * 4 : at + i * 4 + 4, :] = mf[c, i * 16 + my * 4 : i * 16 + my * 4 + 4, :]
            elif axes == (False, False, True):
                stage[c, start : start + 64, :] = nf[c, pl.ds(z, 64, stride=8), :]
                stage[c, at : at + 16, :] = mf[c, pl.ds(mz, 16, stride=4), :]
            elif axes == (True, True, False):
                stage[c, start : start + 8, :] = nf[c, x * 64 + y * 8 : x * 64 + y * 8 + 8, :]
                stage[c, at : at + 4, :] = mf[c, mx * 16 + my * 4 : mx * 16 + my * 4 + 4, :]
            elif axes == (True, False, True):
                stage[c, start : start + 8, :] = nf[c, pl.ds(x * 64 + z, 8, stride=8), :]
                stage[c, at : at + 4, :] = mf[c, pl.ds(mx * 16 + mz, 4, stride=4), :]
            elif axes == (False, True, True):
                stage[c, start : start + 8, :] = nf[c, pl.ds(y * 8 + z, 8, stride=64), :]
                stage[c, at : at + 4, :] = mf[c, pl.ds(my * 4 + mz, 4, stride=16), :]
            else:
                row, mrow = x * 64 + y * 8 + z, mx * 16 + my * 4 + mz
                stage[c, start : start + 1, :] = nf[c, row : row + 1, :]
                stage[c, at : at + 1, :] = mf[c, mrow : mrow + 1, :]
    for rows in (slice(FAR_AT, FAR_AT + FAR_ROWS), slice(0, NEAR_ROWS)):
        packed[rows, :] = jnp.concatenate([stage[0, rows, :], stage[1, rows, :]], axis=1).astype(BF)

    src[MID_AT + 64 : FAR_AT, :] = jnp.zeros((FAR_AT - MID_AT - 64, 256), BF)
    src[FAR_AT + FAR_ROWS : SRC, :] = jnp.zeros((SRC - FAR_AT - FAR_ROWS, 256), BF)
    src[MID_AT : MID_AT + 64, :] = jnp.concatenate([mf[0], mf[1]], axis=1).astype(BF)

    pl.semaphore_wait(barrier, len(greeted))

    z_copies = [
        pltpu.make_async_remote_copy(
            src_ref=zbuf.at[0], dst_ref=zbuf.at[k], send_sem=z_send, recv_sem=z_recv,
            device_id=along_z[k - 1], device_id_type=MESH,
        )
        for k in range(1, 8)
    ]
    def message(i, d):
        rows = pl.ds(*slot(d))
        pair = (far_send, far_recv) if d in FAR else (halo_send, halo_recv)
        return pltpu.make_async_remote_copy(
            src_ref=packed.at[rows], dst_ref=src.at[rows],
            send_sem=pair[0], recv_sem=pair[1], device_id=near[i], device_id_type=MESH,
        )

    for i, d in enumerate(DIRS):
        if i == len(FAR):
            for copy in z_copies:
                copy.start()
        message(i, d).start()

    for load in loads[2:5]:
        load.wait()
    factor = LOG2E / math.sqrt(32)
    lane_head = lax.broadcasted_iota(jnp.int32, (1, 256), 1) // 32
    spread = jnp.zeros((1, 256), F32)
    for h in range(HEADS):
        spread = jnp.where(lane_head == h, scale_ref[h] * factor, spread)
    qn[...] = (dot(normed, wq_ref[...]) * spread).astype(BF)
    turned = dot_t(wq_ref[...].T, normed)
    qm[...] = jnp.zeros_like(qm)
    for h in range(HEADS):
        at = (h % 4) * 32
        qm[h, at : at + 32, :] = (turned[h * 32 : h * 32 + 32, :] * (scale_ref[h] * factor)).astype(BF)
    wvt[...] = wv_ref[...].T
    for part in range(2):
        va[part, :, 32:48, :] = jnp.ones((HEADS, 16, 256), BF)
    ms[...] = jnp.full_like(ms, NEG)
    acc[...] = jnp.zeros_like(acc)

    def wide(rows):
        return jnp.concatenate([nf[0, rows, :], nf[1, rows, :]], axis=1)

    def project(begin, end):
        a = abuf[begin:end, :]
        kbuf[begin:end, :] = dot(a, wk_ref[...]).astype(BF)
        vbuf[begin:end, :] = dot(a, wv_ref[...]).astype(BF)

    loads[5].wait()
    for p in range(1, 4):
        for x in range(8):
            at = x * 64 + (2 * p - 1) * 8
            row = (p * 10 + x + 1) * 16
            abuf[row : row + 16, :] = wide(slice(at, at + 16)).astype(BF)
        project((p * 10 + 1) * 16, (p * 10 + 9) * 16)

    pltpu.make_async_remote_copy(
        src_ref=zbuf.at[pl.ds(1, 7)], dst_ref=zbuf.at[pl.ds(1, 7)], send_sem=z_send, recv_sem=z_recv,
        device_id=along_z[0], device_id_type=MESH,
    ).wait()
    cbuf[0:64, :] = zbuf[...].astype(F32).reshape(64, 256).astype(BF)
    a_copies = [
        pltpu.make_async_remote_copy(
            src_ref=cbuf.at[pl.ds(0, 64)], dst_ref=cbuf.at[pl.ds(64 * k, 64)],
            send_sem=a_send, recv_sem=a_recv, device_id=first[k - 1], device_id_type=MESH,
        )
        for k in range(1, 4)
    ]
    for copy in a_copies:
        copy.start()

    def arrived(begin, count, send_sem, recv_sem):
        rows = pl.ds(begin, count)
        pltpu.make_async_remote_copy(
            src_ref=packed.at[rows], dst_ref=src.at[rows], send_sem=send_sem, recv_sem=recv_sem,
            device_id=near[0], device_id_type=MESH,
        ).wait()

    def cells(d, row):
        start, _ = slot(d)
        at = start + row
        low = at - at % 16
        tile = src[low : low + 16, :].astype(F32)
        return tile[at - low : at - low + 8, :]

    for load in loads[6:]:
        load.wait()
    arrived(0, NEAR_ROWS, halo_send, halo_recv)
    for p in range(1, 4):
        for x, d in ((0, (1, 0, 0)), (9, (-1, 0, 0))):
            at = (2 * p - 1) * 8
            row = (p * 10 + x) * 16
            abuf[row : row + 16, :] = jnp.concatenate([cells(d, at), cells(d, at + 8)], axis=0).astype(BF)
    picked[...] = dot(pick_ref[:, :FAR_AT], src[0:FAR_AT, :])
    project(304, 336)
    project(464, 496)

    arrived(FAR_AT, FAR_ROWS, far_send, far_recv)
    for x in range(10):
        ex = 1 if x == 0 else -1 if x == 9 else 0
        if ex:
            inner = cells((ex, 0, 0), 0), cells((ex, 0, 0), 56)
            outer = cells((ex, 1, 0), 0), cells((ex, -1, 0), 0)
        else:
            at = (x - 1) * 64
            inner = wide(slice(at, at + 8)), wide(slice(at + 56, at + 64))
            outer = cells((0, 1, 0), (x - 1) * 8), cells((0, -1, 0), (x - 1) * 8)
        abuf[x * 16 : x * 16 + 16, :] = jnp.concatenate([outer[0], inner[0]], axis=0).astype(BF)
        abuf[640 + x * 16 : 656 + x * 16, :] = jnp.concatenate([inner[1], outer[1]], axis=0).astype(BF)
    abuf[AT_Z:KEYS, :] = (picked[...] + dot(pick_ref[:, FAR_AT:], src[FAR_AT:SRC, :])).astype(BF)

    pltpu.make_async_remote_copy(
        src_ref=cbuf.at[pl.ds(64, 192)], dst_ref=cbuf.at[pl.ds(64, 192)], send_sem=a_send, recv_sem=a_recv,
        device_id=first[0], device_id_type=MESH,
    ).wait()

    def ring(start, land, count, k, peer):
        return pltpu.make_async_remote_copy(
            src_ref=cbuf.at[pl.ds(start, count)], dst_ref=cbuf.at[pl.ds(land, count)],
            send_sem=b_send, recv_sem=b_recv.at[k], device_id=peer, device_id_type=MESH,
        )

    def swap(k):
        return pltpu.make_async_remote_copy(
            src_ref=cbuf.at[pl.ds(OWN_AT[k], 256)], dst_ref=cbuf.at[pl.ds(SIBLING_AT[k], 256)],
            send_sem=c_send, recv_sem=c_recv.at[k], device_id=partner, device_id_type=MESH,
        )

    ring(0, OWN_AT[1], 256, 1, then[0]).start()
    ring(0, OWN_AT[2], 256, 2, then[1]).start()
    swap(0).start()

    project(0, 176)
    project(624, 1008)
    project(1008, KEYS)

    lane_quad = lax.broadcasted_iota(jnp.int32, (1, 128), 1) // 32
    blank_f, blank_m = jnp.zeros((160, 128), BF), jnp.zeros((96, 128), BF)
    tally = jnp.concatenate(
        [
            jnp.concatenate([jnp.ones((160, 128), BF), blank_m], axis=0),
            jnp.concatenate([blank_f, jnp.ones((96, 128), BF)], axis=0),
        ],
        axis=1,
    )

    def windows(bx, carry):
        mx = lax.div(bx, 2)

        def rows(start, count):
            return pl.ds(pl.multiple_of(start, 16), count)

        def places(by):
            my = by // 2
            parts = [
                rows(by * 160 + bx * 32, 64),
                rows(by * 160 + 160 + bx * 32, 64),
                rows(AT_Z + by * 80 + bx * 16, 32),
                rows(AT_M + my * 96 + mx * 32, 64),
                rows(AT_MZ + my * 48 + mx * 16, 32),
            ]
            return rows(bx * 128 + by * 16, 16), rows(bx * 128 + by * 16 + 64, 16), parts

        def begin(unit):
            r0, r1, parts = places(unit // 2)
            lanes = slice(unit % 2 * 128, unit % 2 * 128 + 128)
            q = jnp.concatenate([qn[r0, lanes], qn[r1, lanes]], axis=0)
            heads = jnp.concatenate([jnp.where(lane_quad == h, q, jnp.zeros_like(q)) for h in range(4)], axis=0)
            keys = jnp.concatenate([kbuf[p, lanes] for p in parts], axis=0)
            wbuf[unit] = dot_t(heads, keys)

        def end(unit):
            r0, r1, parts = places(unit // 2)
            lanes = slice(unit % 2 * 128, unit % 2 * 128 + 128)
            fine = jnp.concatenate([vbuf[p, lanes] for p in parts[:3]] + [blank_m], axis=0)
            mids = jnp.concatenate([blank_f] + [vbuf[p, lanes] for p in parts[3:]], axis=0)
            left = wbuf[unit, :, 0:128].reshape(16, 8, 128)
            right = wbuf[unit, :, 128:256].reshape(16, 8, 128)
            s0 = (left + mask_ref[:, 0:128][None]).reshape(128, 128)
            sf = (right + mask_ref[:, 128:256][None]).reshape(128, 128)
            sm = (right + mask_ref[:, 256:384][None]).reshape(128, 128)
            top_f = jnp.max(jnp.maximum(s0, sf), axis=1, keepdims=True)
            top_m = jnp.max(sm, axis=1, keepdims=True)
            e = jnp.concatenate(
                [jnp.exp2(s0 - top_f), jnp.exp2(jnp.maximum(sf - top_f, sm - top_m))], axis=1
            ).astype(BF)
            mixed = dot(e, jnp.concatenate([fine, mids], axis=1)) / dot(e, tally)
            mixed = mixed[:, :128] + mixed[:, 128:]
            total = mixed[0:32, :]
            for h in range(1, 4):
                total = jnp.where(lane_quad == h, mixed[h * 32 : h * 32 + 32, :], total)
            fm[r0, lanes] = total[:16]
            fm[r1, lanes] = total[16:]

        for unit in range(AHEAD):
            begin(unit)
        for unit in range(8):
            if unit + AHEAD < 8:
                begin(unit + AHEAD)
            end(unit)
        return carry

    lax.fori_loop(0, 4, windows, 0)

    ring(0, OWN_AT[1], 256, 1, then[0]).wait_recv()
    ring(OWN_AT[1], OWN_AT[3], 128, 3, then[0]).start()
    ring(0, OWN_AT[2], 256, 2, then[1]).wait_recv()
    ring(OWN_AT[2] + 128, OWN_AT[3] + 128, 128, 3, then[1]).start()
    swap(1).start()
    swap(2).start()

    def scores_of(unit):
        part, h = unit // HEADS, unit % HEADS
        s = dot(kc[part, h // 4], qm[h])
        held[unit] = s
        return jnp.max(s.reshape(32, 8, 512), axis=0)

    def absorb(unit, block_top):
        part, h = unit // HEADS, unit % HEADS
        old = ms[h]
        top = jnp.maximum(old, jnp.max(block_top, axis=0, keepdims=True))
        p = jnp.exp2(held[unit] - top).astype(BF)
        acc[h] = acc[h] * jnp.exp2(old - top) + dot(va[part, h], p)
        ms[h] = top

    def coarse_block(j, carry):
        @pl.when(j == 0)
        def _():
            swap(0).wait_recv()

        @pl.when(j == 2)
        def _():
            ring(0, OWN_AT[3], 256, 3, then[0]).wait_recv()
            swap(3).start()
            swap(1).wait_recv()
            swap(2).wait_recv()

        @pl.when(j == 3)
        def _():
            swap(3).wait_recv()

        def block(part):
            return pl.ds(pl.multiple_of(j * 512 + part * 256, 256), 256)

        def project_keys(part):
            k = dot(cbuf[block(part), :], wk_ref[...]).astype(BF)
            kc[part, 0] = k[:, :128]
            kc[part, 1] = k[:, 128:]

        def project_values(part):
            v = dot_t(wvt[...], cbuf[block(part), :]).astype(BF)
            for h in range(HEADS):
                va[part, h, 0:32, :] = v[h * 32 : h * 32 + 32, :]

        project_keys(0)
        tops = [scores_of(h) for h in range(3)]
        project_values(0)
        for unit in range(2 * HEADS):
            if unit == 2:
                project_keys(1)
            if unit == 4:
                project_values(1)
            if unit + 3 < 2 * HEADS:
                tops.append(scores_of(unit + 3))
            absorb(unit, tops[unit])
        return carry

    lax.fori_loop(0, 4, coarse_block, 0)

    turned_out = jnp.concatenate([acc[h, 0:32, :] / acc[h, 32:33, :] for h in range(HEADS)], axis=0)
    out_ref[...] = (fm[...] + turned_out.T).astype(BF)

    pltpu.make_async_remote_copy(
        src_ref=cbuf.at[pl.ds(256, 768)], dst_ref=cbuf.at[pl.ds(256, 768)], send_sem=b_send, recv_sem=b_recv.at[0],
        device_id=then[0], device_id_type=MESH,
    ).wait_send()
    pltpu.make_async_remote_copy(
        src_ref=cbuf.at[pl.ds(0, 1024)], dst_ref=cbuf.at[pl.ds(0, 1024)], send_sem=c_send, recv_sem=c_recv.at[0],
        device_id=partner, device_id_type=MESH,
    ).wait_send()


def finish_kernel(att_ref, tok_ref, wo_ref, gain2_ref, up_ref, down_ref, out_hbm, out_ref, sems):
    parts = [slice(i * 128, i * 128 + 128) for i in range(4)]
    residuals = [(tok_ref[p, :].astype(F32) + dot(att_ref[p, :], wo_ref[...])).astype(BF) for p in parts]
    copies = []
    for i, (p, residual) in enumerate(zip(parts, residuals)):
        wide = residual.astype(F32)
        u = dot(normalized(wide, gain2_ref[...]), up_ref[...])
        inner = u * (GELU + (GELU * 0.044715) * (u * u))
        half = 0.5 * u
        hidden = (half + half * jnp.tanh(inner)).astype(BF)
        out_ref[p, :] = (wide + dot(hidden, down_ref[...])).astype(BF)
        copies.append(pltpu.make_async_copy(out_ref.at[pl.ds(i * 128, 128)], out_hbm.at[pl.ds(i * 128, 128)], sems.at[i]))
        copies[-1].start()
    for copy in copies:
        copy.wait()


def shards(
    tokens, norm_gain, query_weight, key_weight, value_weight, head_scale, out_weight, mlp_gain, up_weight, down_weight
):
    shape = tokens.shape
    vmem = pl.BlockSpec(memory_space=pltpu.VMEM)
    hbm = pl.BlockSpec(memory_space=pltpu.MemorySpace.HBM)
    dma = pltpu.SemaphoreType.DMA
    V = pltpu.VMEM
    flat_tokens = tokens.reshape(512, 256)
    attended = pl.pallas_call(
        layer_kernel,
        out_shape=jax.ShapeDtypeStruct((512, 256), BF),
        in_specs=[hbm] * 8,
        out_specs=vmem,
        scratch_shapes=[
            V((2, 512, 128), F32),
            V((2, 64, 128), F32),
            V((2, 128, 128), F32),
            V((2, 32, 128), F32),
            V((2, SRC, 128), F32),
            V((SRC, 256), BF),
            V((SRC, 256), BF),
            V((8, 8, 256), BF),
            V((2048, 256), BF),
            V((KEYS, 256), BF),
            V((512, 256), BF),
            V((8, 128, 512), BF),
            V((KEYS, 256), BF),
            V((KEYS, 256), BF),
            V((8, 128, 256), F32),
            V((512, 256), F32),
            V((2, 2, 256, 128), BF),
            V((2, 8, 48, 256), BF),
            V((16, 256, 512), F32),
            V((8, 1, 512), F32),
            V((8, 48, 512), F32),
            V((512, 256), BF),
            V((1, 256), F32),
            V((256, 256), BF),
            V((256, 256), BF),
            V((256, 256), BF),
            pltpu.SMEM((8,), F32),
            V((KEYS - AT_Z, SRC), BF),
            V((8, 384), F32),
            V((256, 256), BF),
            V((KEYS - AT_Z, 256), F32),
            dma((8,)),
            dma,
            dma,
            dma,
            dma,
            dma,
            dma,
            dma,
            dma,
            dma,
            dma((4,)),
            dma,
            dma((4,)),
        ],
        compiler_params=pltpu.CompilerParams(
            collective_id=0, has_side_effects=True, vmem_limit_bytes=28 << 20
        ),
        name="layer",
    )(
        *(
            pltpu.with_memory_space_constraint(a, pltpu.MemorySpace.HBM)
            for a in (
                flat_tokens,
                norm_gain.reshape(1, 256),
                query_weight,
                key_weight,
                value_weight,
                head_scale,
                jnp.asarray(selection(), BF),
                jnp.asarray(window_masks()),
            )
        )
    )
    flat = pl.pallas_call(
        finish_kernel,
        out_shape=jax.ShapeDtypeStruct((512, 256), BF),
        in_specs=[vmem] * 6,
        out_specs=pl.BlockSpec(memory_space=pl.ANY),
        scratch_shapes=[V((512, 256), BF), dma((4,))],
        compiler_params=pltpu.CompilerParams(vmem_limit_bytes=12 << 20),
        name="finish",
    )(attended, flat_tokens, out_weight, mlp_gain.reshape(1, 256), up_weight, down_weight)
    return flat.reshape(shape)


def solution(mesh):
    in_specs = (P("gx", "gy", "gz", None), P(), P(), P(), P(), P(), P(), P(), P(), P())
    step = jax.shard_map(shards, mesh=mesh, in_specs=in_specs, out_specs=P("gx", "gy", "gz", None), check_vma=False)

    def traced(*arguments):
        with jax.sharding.use_abstract_mesh(mesh.abstract_mesh):
            return step(*arguments)

    return traced
```
